32 devices in a mesh: wide: 8 (over z, y), narrow: 4 (over x, core).
Axes of the slice: x: 2, y: 2, z: 4, core: 2. Of those that a mesh axis runs over, the one named last changes fastest.
Arguments:
- tokens: bfloat16 [8192, 2048], P(('wide', 'narrow')), may hold values from -6 to 6
- out_grad: bfloat16 [8192, 2048], P(('wide', 'narrow')), may hold values from -6 to 6
- attn_norm: bfloat16 [2048], P(('wide', 'narrow')), may hold values from 0.099609375 to 1.8984375
- w_query: bfloat16 [2048, 2048], P(('wide', 'narrow')), may hold values from -0.125 to 0.125
- key_weight: bfloat16 [2048, 1024], P(('wide', 'narrow')), may hold values from -0.125 to 0.125
- value_weight: bfloat16 [2048, 1024], P(('wide', 'narrow')), may hold values from -0.125 to 0.125
- query_norm: bfloat16 [128], P(('wide', 'narrow')), may hold values from 0.099609375 to 1.8984375
- key_norm_gain: bfloat16 [128], P(('wide', 'narrow')), may hold values from 0.099609375 to 1.8984375
- w_out: bfloat16 [2048, 2048], P(('wide', 'narrow')), may hold values from -0.75 to 0.75
- mlp_norm: bfloat16 [2048], P(('wide', 'narrow')), may hold values from 0.099609375 to 1.8984375
- w_gate: bfloat16 [2048, 6144], P(('wide', 'narrow')), may hold values from -0.125 to 0.125
- w_up: bfloat16 [2048, 6144], P(('wide', 'narrow')), may hold values from -0.125 to 0.125
- w_down: bfloat16 [6144, 2048], P(('wide', 'narrow')), may hold values from -0.078125 to 0.078125
- doc_blocks: int32 [4, 8], replicated, may hold values from 1 to 4, 16 in all within a row
- doc_tail: int32 [4, 8], replicated, may hold values from 1 to 128
- doc_order: int32 [4, 8], replicated, may hold values from 0 to 7, each once within a row
- block_home: int32 [4, 8], replicated, may hold values from 0 to 7, each once within a row
Outputs:
- output: bfloat16 [8192, 2048], P(('wide', 'narrow'))
- tokens_grad: bfloat16 [8192, 2048], P(('wide', 'narrow'))
- attn_norm_grad: float32 [2048], P(('wide', 'narrow'))
- w_query_grad: float32 [2048, 2048], P(('wide', 'narrow'))
- w_key_grad: float32 [2048, 1024], P(('wide', 'narrow'))
- w_value_grad: float32 [2048, 1024], P(('wide', 'narrow'))
- query_norm_grad: float32 [128], P(('wide', 'narrow'))
- key_norm_grad: float32 [128], P(('wide', 'narrow'))
- w_out_grad: float32 [2048, 2048], P(('wide', 'narrow'))
- mlp_norm_grad: float32 [2048], P(('wide', 'narrow'))
- w_gate_grad: float32 [2048, 6144], P(('wide', 'narrow'))
- w_up_grad: float32 [2048, 6144], P(('wide', 'narrow'))
- w_down_grad: float32 [6144, 2048], P(('wide', 'narrow'))
The draws below stay inside these ranges and needn't reach their ends.
Inputs may be any that keep to these rules, and one draw needn't show every extreme that they name: Owner o of narrow group n gets one document of doc_blocks[n, o] blocks; each row sums to 16, and in each row some owner gets 4. `doc_order`: each row is a permutation of the owners. `block_home`: each row is a permutation of the wide indices.
All inputs are finite; a program needn't handle non-finite values.
Results may differ from the reference program's by a relative error of at most 0.019.
Values may be sent and summed in bfloat16 or wider, within the bound.
No kernel may reach another device: no remote copies, remote signals or barrier semaphores. Data moves between devices by JAX's collectives and lax.ppermute only.
A program may use at most 448 MiB of HBM per device.

```python
import math
import jax
import jax.numpy as jnp
import numpy as np
from jax import lax

MODEL_WIDTH = 2048
QUERY_HEADS = 16
KEY_VALUE_HEADS = 8
HEAD_WIDTH = 128
FF = 6144
BLK = 128
OWN_BLK = 4
NBLK = 2
OWNERS = 8
GROUPS = 4
BLOCKS = 16
TOKEN_ROWS = 8192


def touch_ends(values, key, least, top_value):
    longest = values.shape.index(max(values.shape))
    spots = []
    for shift in (0, 1):
        where = [jax.random.randint(jax.random.fold_in(key, axis), (), 0, length) for axis, length in enumerate(values.shape)]
        where[longest] = (where[longest] + shift) % values.shape[longest]
        spots.append(tuple(where))
    return values.at[spots[0]].set(least).at[spots[1]].set(top_value)


def block_levels(stream_key, extent, pieces, least, high):
    def one(position, blocks):
        draws = jax.random.uniform(jax.random.fold_in(jax.random.fold_in(stream_key, 6), position), (blocks,), jnp.float32, least / len(pieces), high / len(pieces))
        return jnp.repeat(jnp.exp(draws), extent[position] // blocks).reshape((-1,) + (1,) * (len(extent) - position - 1))

    gain = one(*pieces[0])
    for cut in pieces[1:]:
        gain = gain * one(*cut)
    return gain


def profile(number_of, total, bound, lean):
    loads = [(1 << 20) // math.isqrt(standing ** lean) + 1 for standing in range(2, number_of + 1)]
    rest, holding = total - bound - (number_of - 1), [1] * (number_of - 1)
    while rest > 0:
        candidates = [i for i in range(number_of - 1) if holding[i] < bound]
        mass, remaining = sum([loads[i] for i in candidates]), rest
        for i in candidates:
            addition = min(bound - holding[i], max(1, remaining * loads[i] // mass), rest)
            holding[i] = holding[i] + addition
            rest = rest - addition
    return np.array([bound] + holding)


def uneven(rng, count, total, most, lean):
    if count == 2:
        one = jax.random.randint(rng, (), max(1, total - most), min(most, total - 1) + 1)
        return jnp.stack([one, total - one])
    sizes = jnp.asarray(profile(count, total, most, lean), jnp.int32)
    pairs = (count - 1) // 2
    giver, sink = sizes[1:1 + 2 * pairs:2], sizes[2:2 + 2 * pairs:2]
    room = jnp.minimum(giver - 1, most - sink)
    moved = jax.random.randint(jax.random.fold_in(rng, 1), (pairs,), 0, 1 << 20) % (room + 1)
    sizes = sizes.at[1:1 + 2 * pairs:2].set(giver - moved).at[2:2 + 2 * pairs:2].set(sink + moved)
    return sizes[jax.random.permutation(jax.random.fold_in(rng, 2), count)]


def centred(key, shape, deviation, limit, split=(), kind=jnp.bfloat16):
    values = jax.random.normal(key, shape, jnp.float32) * deviation
    if len(split) > 0:
        values = block_levels(key, shape, split, -0.22, 0.18) * values
    return jnp.clip(values, min=-limit, max=limit).astype(kind)


def setup_inputs(seed: int = 0) -> dict:
    arg_keys = jax.random.split(jax.random.key(seed), 18)
    tokens = centred(arg_keys[0], (TOKEN_ROWS, MODEL_WIDTH), 1.0, 6.0, ((0, 32),))
    out_grad = centred(arg_keys[1], (TOKEN_ROWS, MODEL_WIDTH), 1.0, 6.0, ((0, 32),))
    attn_norm = jnp.clip(1.0 + 0.18 * jax.random.normal(arg_keys[2], (MODEL_WIDTH,), jnp.float32), 0.099609375, 1.8984375).astype(jnp.bfloat16)
    w_query = centred(arg_keys[3], (MODEL_WIDTH, QUERY_HEADS * HEAD_WIDTH), MODEL_WIDTH ** -0.5, 0.125, ((0, 32),))
    key_weight = centred(arg_keys[4], (MODEL_WIDTH, KEY_VALUE_HEADS * HEAD_WIDTH), MODEL_WIDTH ** -0.5, 0.125, ((0, 32),))
    value_weight = centred(arg_keys[5], (MODEL_WIDTH, KEY_VALUE_HEADS * HEAD_WIDTH), MODEL_WIDTH ** -0.5, 0.125, ((0, 32),))
    query_norm = jnp.clip(1.0 + 0.18 * jax.random.normal(arg_keys[6], (HEAD_WIDTH,), jnp.float32), 0.099609375, 1.8984375).astype(jnp.bfloat16)
    key_norm_gain = jnp.clip(1.0 + 0.18 * jax.random.normal(arg_keys[7], (HEAD_WIDTH,), jnp.float32), 0.099609375, 1.8984375).astype(jnp.bfloat16)
    w_out = centred(arg_keys[8], (QUERY_HEADS * HEAD_WIDTH, MODEL_WIDTH), (QUERY_HEADS * HEAD_WIDTH // 32) ** -0.5, 0.75, ((0, 32),))
    mlp_norm = jnp.clip(1.0 + 0.18 * jax.random.normal(arg_keys[9], (MODEL_WIDTH,), jnp.float32), 0.099609375, 1.8984375).astype(jnp.bfloat16)
    w_gate = centred(arg_keys[10], (MODEL_WIDTH, FF), MODEL_WIDTH ** -0.5, 0.125, ((0, 32),))
    w_up = centred(arg_keys[11], (MODEL_WIDTH, FF), MODEL_WIDTH ** -0.5, 0.125, ((0, 32),))
    w_down = centred(arg_keys[12], (FF, MODEL_WIDTH), FF ** -0.5, 0.078125, ((0, 32),))
    doc_blocks = jax.vmap(lambda own: uneven(own, OWNERS, BLOCKS, OWN_BLK, 2))(jax.random.split(arg_keys[13], GROUPS)).reshape((GROUPS, OWNERS)).astype(jnp.int32)
    doc_tail = touch_ends(jax.random.randint(arg_keys[14], (GROUPS, OWNERS), 1, BLK + 1), jax.random.fold_in(arg_keys[14], 1), 1, BLK).astype(jnp.int32)
    doc_order = jax.vmap(lambda own: jax.random.permutation(own, OWNERS))(jax.random.split(arg_keys[15], GROUPS)).reshape((GROUPS, OWNERS)).astype(jnp.int32)
    block_home = jax.vmap(lambda own: jax.random.permutation(own, OWNERS))(jax.random.split(arg_keys[16], GROUPS)).reshape((GROUPS, OWNERS)).astype(jnp.int32)
    return dict(tokens=tokens, out_grad=out_grad, attn_norm=attn_norm, w_query=w_query, key_weight=key_weight, value_weight=value_weight, query_norm=query_norm, key_norm_gain=key_norm_gain, w_out=w_out, mlp_norm=mlp_norm, w_gate=w_gate, w_up=w_up, w_down=w_down, doc_blocks=doc_blocks, doc_tail=doc_tail, doc_order=doc_order, block_home=block_home)


EPSILON = 1e-06
THETA = 1000000.0
TOP_PRECISION = lax.Precision.HIGHEST

@jax.custom_vjp
def lower_precision(v):
    return lax.optimization_barrier(v.astype(jnp.bfloat16)).astype(jnp.float32)

@jax.custom_vjp
def lower_precision_backward(v):
    return v

def low_keep(v):
    return (lower_precision(v), None)

def low_pass(kept, grad):
    return (grad,)

def back_keep(v):
    return (v, None)

def back_low(kept, grad):
    return (lower_precision(grad),)
lower_precision.defvjp(low_keep, low_pass)
lower_precision_backward.defvjp(back_keep, back_low)

def row_normalize(values, gain_row):
    return values * lax.rsqrt(lax.optimization_barrier(jnp.mean(values * values, axis=-1, keepdims=True)) + EPSILON) * gain_row

def apply_rotary(values, token_position):
    half_size = values.shape[-1] // 2
    frequency = THETA ** (-2.0 * jnp.arange(half_size, dtype=jnp.float32) / values.shape[-1])
    angles = token_position.astype(jnp.float32)[:, None] * frequency[None, :]
    angles = jnp.concatenate([angles, angles], axis=-1)[:, None, :]
    turned = jnp.concatenate([-values[..., half_size:], values[..., :half_size]], axis=-1)
    return values * jnp.cos(angles) + turned * jnp.sin(angles)

def layout(doc_blocks, doc_tail, doc_order, block_home):
    owner_ids = jnp.arange(OWNERS, dtype=jnp.int32)
    order_hits = (doc_order[:, :, None] == owner_ids[None, None, :]).astype(jnp.int32)
    in_stream = lax.optimization_barrier(jnp.sum(order_hits * doc_blocks[:, None, :], axis=2))
    stream_start = jnp.cumsum(in_stream, axis=1) - in_stream
    owner_start = lax.optimization_barrier(jnp.sum(order_hits * stream_start[:, :, None], axis=1))
    slot_ids = jnp.arange(OWN_BLK, dtype=jnp.int32)
    blocks = owner_start[:, :, None] + slot_ids[None, None, :]
    columns = blocks % OWNERS
    column_hits = columns[..., None] == owner_ids
    home_ids = lax.optimization_barrier(jnp.sum(jnp.where(column_hits, block_home[:, None, None, :], 0), axis=-1))
    group_ids = jnp.arange(GROUPS, dtype=jnp.int32)[:, None, None]
    first_rows = ((home_ids * GROUPS + group_ids) * NBLK + blocks // OWNERS) * BLK
    present = slot_ids[None, None, :] < doc_blocks[:, :, None]
    row_index = first_rows[..., None] + jnp.arange(BLK, dtype=jnp.int32)
    row_index = jnp.where(present[..., None], row_index, TOKEN_ROWS)
    lengths = (doc_blocks - 1) * BLK + doc_tail
    return (row_index.reshape(GROUPS * OWNERS, OWN_BLK * BLK), lengths.reshape(GROUPS * OWNERS))

def attend_doc(packed_rows, doc_length):
    document_extent = packed_rows.shape[0]
    query_rows = packed_rows[:, :QUERY_HEADS * HEAD_WIDTH].reshape(document_extent, KEY_VALUE_HEADS, QUERY_HEADS // KEY_VALUE_HEADS, HEAD_WIDTH)
    key_row_block = packed_rows[:, QUERY_HEADS * HEAD_WIDTH:(QUERY_HEADS + KEY_VALUE_HEADS) * HEAD_WIDTH].reshape(document_extent, KEY_VALUE_HEADS, HEAD_WIDTH)
    value_row_block = packed_rows[:, (QUERY_HEADS + KEY_VALUE_HEADS) * HEAD_WIDTH:].reshape(document_extent, KEY_VALUE_HEADS, HEAD_WIDTH)
    places = jnp.arange(document_extent, dtype=jnp.int32)
    allowed = (places[None, :] <= places[:, None]) & (places[None, :] < doc_length)
    scores = lower_precision_backward(jnp.einsum('qgec,kgc->geqk', query_rows, key_row_block, precision=TOP_PRECISION) * HEAD_WIDTH ** (-0.5))
    scores = jnp.where(allowed, scores, -1e+30)
    weights = lower_precision(jax.nn.softmax(scores, axis=-1))
    mixed_rows = jnp.einsum('geqk,kgc->qgec', weights, value_row_block, precision=TOP_PRECISION)
    return mixed_rows.reshape(document_extent, QUERY_HEADS * HEAD_WIDTH)

def attend_pair(items):
    return attend_doc(items[0], items[1])

def forward(inputs, attn_norm, w_query, key_weight, value_weight, query_norm, key_norm_gain, w_out, mlp_norm, w_gate, w_up, w_down, row_index, lengths, token_position):
    normalized_rows = lower_precision(row_normalize(inputs, attn_norm))
    query_raw = lower_precision_backward(jnp.dot(normalized_rows, w_query, precision=TOP_PRECISION)).reshape(TOKEN_ROWS, QUERY_HEADS, HEAD_WIDTH)
    key_unscaled = lower_precision_backward(jnp.dot(normalized_rows, key_weight, precision=TOP_PRECISION)).reshape(TOKEN_ROWS, KEY_VALUE_HEADS, HEAD_WIDTH)
    value_row_block = lower_precision(lower_precision_backward(jnp.dot(normalized_rows, value_weight, precision=TOP_PRECISION)))
    query_rows = lower_precision(lower_precision_backward(apply_rotary(row_normalize(query_raw, query_norm), token_position).reshape(TOKEN_ROWS, QUERY_HEADS * HEAD_WIDTH)))
    key_row_block = lower_precision(lower_precision_backward(apply_rotary(row_normalize(key_unscaled, key_norm_gain), token_position).reshape(TOKEN_ROWS, KEY_VALUE_HEADS * HEAD_WIDTH)))
    packed_rows = jnp.concatenate([query_rows, key_row_block, value_row_block], axis=1)
    documents = jnp.take(packed_rows, jnp.minimum(row_index, TOKEN_ROWS - 1), axis=0)
    attended = lax.map(jax.checkpoint(attend_pair), (documents, lengths))
    attended = lower_precision(lower_precision_backward(attended))
    present = (row_index < TOKEN_ROWS)[..., None]
    gathered = jnp.zeros((TOKEN_ROWS, QUERY_HEADS * HEAD_WIDTH), jnp.float32).at[row_index].add(jnp.where(present, attended, 0.0), mode='drop')
    middle = inputs + lower_precision_backward(jnp.dot(gathered, w_out, precision=TOP_PRECISION))
    normed_two = lower_precision(row_normalize(middle, mlp_norm))
    gate_sum = lower_precision_backward(jnp.dot(normed_two, w_gate, precision=TOP_PRECISION))
    up_sum = lower_precision_backward(jnp.dot(normed_two, w_up, precision=TOP_PRECISION))
    hidden = lower_precision(jax.nn.silu(gate_sum) * up_sum)
    return middle + lower_precision_backward(jnp.dot(hidden, w_down, precision=TOP_PRECISION))

def reference(tokens, out_grad, attn_norm, w_query, key_weight, value_weight, query_norm, key_norm_gain, w_out, mlp_norm, w_gate, w_up, w_down, doc_blocks, doc_tail, doc_order, block_home):
    row_index, lengths = layout(doc_blocks, doc_tail, doc_order, block_home)
    places = jnp.broadcast_to(jnp.arange(OWN_BLK * BLK, dtype=jnp.int32)[None, :], row_index.shape).reshape(-1)
    token_position = jnp.zeros((TOKEN_ROWS,), jnp.int32).at[row_index.reshape(-1)].set(places, mode='drop')
    params = (attn_norm, w_query, key_weight, value_weight, query_norm, key_norm_gain, w_out, mlp_norm, w_gate, w_up, w_down)
    floats = tuple((matrix.astype(jnp.float32) for matrix in params))

    def closed(inputs, gain_one, query_w, key_w, value_w, query_gain, key_gain, out_w, gain_two, gate_w, up_w, down_w):
        return forward(inputs, gain_one, query_w, key_w, value_w, query_gain, key_gain, out_w, gain_two, gate_w, up_w, down_w, row_index, lengths, token_position)
    result, pullback = jax.vjp(closed, tokens.astype(jnp.float32), *floats)
    grads = pullback(out_grad.astype(jnp.float32))
    return (result.astype(jnp.bfloat16), grads[0].astype(jnp.bfloat16), grads[1], grads[2], grads[3], grads[4], grads[5], grads[6], grads[7], grads[8], grads[9], grads[10], grads[11])
```

```python
import functools

import jax
import jax.numpy as jnp
import numpy as np
from jax import lax
from jax.experimental import pallas as pl
from jax.experimental.pallas import tpu as pltpu
from jax.sharding import PartitionSpec as P

BLK = 128
OWN_BLK = 4
EPSILON = 1e-06
THETA = 1000000.0
LANES = 128
NARROW = 4
CONTRACT_ROWS = (((0,), (0,)), ((), ()))
CONTRACT_COLS = (((1,), (1,)), ((), ()))
NEGATIVE = -1e30
F32 = jnp.float32
BF16 = jnp.bfloat16
DEVICES = ("wide", "narrow")


def row_normalize(values, gain_row):
    return (
        values * lax.rsqrt(jnp.mean(values * values, axis=-1, keepdims=True) + EPSILON) * gain_row
    )


def apply_rotary(values, cosines, sines):
    half_size = values.shape[-1] // 2
    turned = jnp.concatenate([-values[..., half_size:], values[..., :half_size]], axis=-1)
    return values * cosines[:, None, :] + turned * sines[:, None, :]


def finish_heads(raw, scale, cosines, sines):
    rows = raw.shape[0]
    heads = raw.reshape(rows, -1, scale.shape[0])
    return apply_rotary(row_normalize(heads, scale), cosines, sines).reshape(rows, -1)


def gated(gate_sum, up_sum):
    return jax.nn.silu(gate_sum) * up_sum


def dot(left, right):
    return jnp.dot(left, right, preferred_element_type=F32)


def outer_sum(left_rows, right_rows):
    return lax.dot_general(left_rows, right_rows, CONTRACT_ROWS, preferred_element_type=F32)


def times_transpose(left_rows, matrix):
    return lax.dot_general(left_rows, matrix, CONTRACT_COLS, preferred_element_type=F32)


def ring_order(count):
    rows = count // 2
    return [2 * i for i in range(rows)] + [2 * i + 1 for i in reversed(range(rows))]


class Ring:
    def __init__(self, count):
        self.count = count
        order = ring_order(count)
        place = np.zeros(count, np.int32)
        for i, device in enumerate(order):
            place[device] = i
        self.onward = [(order[i], order[(i + 1) % count]) for i in range(count)]
        self.back = [(b, a) for a, b in self.onward]
        self.order = jnp.asarray(np.array(order + order + order, np.int32))
        self.place = jnp.asarray(place)[lax.axis_index("wide")]

    def device(self, shift):
        return self.order[self.place + self.count + shift]

    def send(self, value, forward):
        return lax.ppermute(value, "wide", self.onward if forward else self.back)


def no_op(out_ref):
    pass


def blank(shape, dtype):
    return pl.pallas_call(
        no_op,
        out_shape=jax.ShapeDtypeStruct(shape, dtype),
        out_specs=pl.BlockSpec(memory_space=pl.ANY),
    )()


def ring_gather(ring, part):
    if ring.count > 8:
        return lax.all_gather(part, "wide", axis=0, tiled=True)
    rows, cols = part.shape
    half = rows // 2
    whole = blank((ring.count * rows, cols), part.dtype)

    def put(whole, value, shift, extra):
        return lax.dynamic_update_slice(whole, value, (ring.device(shift) * rows + extra, 0))

    whole = put(whole, part, 0, 0)
    ahead, behind = part, part
    for step in range(1, ring.count // 2):
        ahead, behind = ring.send(ahead, True), ring.send(behind, False)
        whole = put(put(whole, ahead, -step, 0), behind, step, 0)
    last = ring.count // 2
    whole = put(whole, ring.send(ahead[:half], True), -last, 0)
    return put(whole, ring.send(behind[half:], False), last, half)


def ring_reduce(ring, terms):
    if ring.count > 8:
        return lax.psum_scatter(terms, "wide", scatter_dimension=0, tiled=True).astype(F32)
    rows = terms.shape[0] // ring.count
    cols = terms.shape[1]
    half = rows // 2

    def term(shift):
        return lax.dynamic_slice(terms, (ring.device(shift) * rows, 0), (rows, cols))

    last = ring.count // 2
    far = term(last)
    ahead, behind = ring.send(far[:half], True), ring.send(far[half:], False)
    for step in range(last - 1, 0, -1):
        mine, other = term(step), term(-step)
        if step == last - 1:
            ahead = jnp.concatenate([join(mine[:half], ahead), mine[half:]], axis=0)
            behind = jnp.concatenate([other[:half], join(other[half:], behind)], axis=0)
        else:
            ahead, behind = join(mine, ahead), join(other, behind)
        ahead, behind = ring.send(ahead, True), ring.send(behind, False)
    return term(0).astype(F32) + ahead.astype(F32) + behind.astype(F32)


def join(left, right):
    return (left.astype(F32) + right.astype(F32)).astype(BF16)


def swap(value, bit):
    return lax.ppermute(value, "narrow", [(i, i ^ bit) for i in range(NARROW)])


def narrow_gather(value):
    across = swap(value, 2)
    return jnp.concatenate([value, swap(value, 1), across, swap(across, 1)], axis=0)


def narrow_reduce(terms):
    rows = terms.shape[0] // NARROW
    low = terms.astype(BF16)
    parts = [low[i * rows : (i + 1) * rows] for i in range(NARROW)]
    near, far = swap(parts[1], 1), swap(parts[3], 1)
    across = swap(join(parts[2], far), 2)
    return parts[0].astype(F32) + near.astype(F32) + across.astype(F32)


def everyone_sum(vector, wide_count):
    for bit in (1, 2):
        vector = vector + swap(vector, bit)
    bit = 1
    while bit < wide_count:
        vector = vector + lax.ppermute(
            vector, "wide", [(i, i ^ bit) for i in range(wide_count)]
        )
        bit *= 2
    return vector


def layout(doc_blocks, doc_order, block_home, my_wide, block_count):
    owners = doc_blocks.shape[1]
    owner_ids = jnp.arange(owners, dtype=jnp.int32)
    hits = (doc_order[:, :, None] == owner_ids[None, None, :]).astype(jnp.int32)
    in_stream = jnp.sum(hits * doc_blocks[:, None, :], axis=2)
    before = (owner_ids[:, None] < owner_ids[None, :]).astype(jnp.int32)
    stream_start = jnp.sum(in_stream[:, :, None] * before[None], axis=1)
    owner_start = jnp.sum(hits * stream_start[:, :, None], axis=1)
    column = jnp.sum(jnp.where(block_home == my_wide, owner_ids[None, :], 0), axis=1)
    stream_ids = jnp.arange(block_count, dtype=jnp.int32)[None, :] * owners + column[:, None]
    member = (owner_start[:, None, :] <= stream_ids[:, :, None]) & (
        stream_ids[:, :, None] < (owner_start + doc_blocks)[:, None, :]
    )
    offsets = stream_ids - jnp.sum(jnp.where(member, owner_start[:, None, :], 0), axis=2)
    return owner_start, offsets


def stream_table(group, owner_start, doc_blocks, doc_tail, block_home, block_count):
    def pick(table):
        return lax.dynamic_index_in_dim(table, group, 0, keepdims=False)

    starts, blocks, tails, homes = pick(owner_start), pick(doc_blocks), pick(doc_tail), pick(block_home)
    owners = starts.shape[0]
    ids = jnp.arange(owners * block_count, dtype=jnp.int32)
    member = (starts[None, :] <= ids[:, None]) & (ids[:, None] < (starts + blocks)[None, :])

    def chosen(values):
        return jnp.sum(jnp.where(member, values[None, :], 0), axis=1)

    home = jnp.sum(
        jnp.where(
            (ids % owners)[:, None] == jnp.arange(owners, dtype=jnp.int32)[None, :],
            homes[None, :],
            0,
        ),
        axis=1,
    )
    place = home * block_count + ids // owners
    return jnp.stack([place, chosen(starts), chosen((blocks - 1) * BLK + tails)])


def window(table, rows_ref, b, heads, size):
    first, length = table[1, b], table[2, b]
    width = heads * size
    mine = rows_ref[pl.ds(pl.multiple_of(table[0, b] * BLK, BLK), BLK), :width]
    queries = jnp.concatenate([mine[:, i * size : (i + 1) * size] for i in range(heads)], axis=0)
    spot = (b - first) * BLK
    row = lax.broadcasted_iota(jnp.int32, (heads, BLK, BLK), 1).reshape(heads * BLK, BLK) + spot
    col = lax.broadcasted_iota(jnp.int32, (heads * BLK, BLK), 1) + spot
    starts, keys, values, scores = [], [], [], []
    for i in range(OWN_BLK):
        start = pl.multiple_of(table[0, jnp.maximum(b - i, 0)] * BLK, BLK)
        key = rows_ref[pl.ds(start, BLK), width : width + size]
        col_i = col - i * BLK
        allowed = (col_i <= row) & (col_i < length) & (col_i >= 0)
        score = times_transpose(queries, key) * size ** (-0.5)
        starts.append(start)
        keys.append(key)
        values.append(rows_ref[pl.ds(start, BLK), width + size : width + 2 * size])
        scores.append(jnp.where(allowed, score, NEGATIVE))
    highest = scores[0]
    for score in scores[1:]:
        highest = jnp.maximum(highest, score)
    highest = jnp.max(highest, axis=-1, keepdims=True)
    powers = [jnp.exp(score - highest) for score in scores]
    total = powers[0]
    for power in powers[1:]:
        total = total + power
    total = jnp.sum(total, axis=-1, keepdims=True)
    weights = [power / total for power in powers]
    return mine, queries, starts, keys, values, weights


def forward_kernel(heads, size, table, rows_ref, out_ref):
    def step(b, carry):
        _, _, starts, _, values, weights = window(table, rows_ref, b, heads, size)
        mixed = dot(weights[0].astype(BF16), values[0])
        for weight, value in zip(weights[1:], values[1:]):
            mixed = mixed + dot(weight.astype(BF16), value)
        for i in range(heads):
            out_ref[pl.ds(starts[0], BLK), i * size : (i + 1) * size] = mixed[
                i * BLK : (i + 1) * BLK
            ].astype(BF16)
        return carry

    lax.fori_loop(0, table.shape[1], step, 0)


def backward_kernel(heads, size, table, rows_ref, grad_ref, out_ref, sums):
    sums[...] = jnp.zeros_like(sums)
    scale = size ** (-0.5)

    def step(b, carry):
        _, queries, starts, keys, values, weights = window(table, rows_ref, b, heads, size)
        grads = grad_ref[pl.ds(starts[0], BLK), :]
        grads = jnp.concatenate([grads[:, i * size : (i + 1) * size] for i in range(heads)], axis=0)
        pulls = [times_transpose(grads, value) for value in values]
        total = weights[0] * pulls[0]
        for weight, pull in zip(weights[1:], pulls[1:]):
            total = total + weight * pull
        total = jnp.sum(total, axis=-1, keepdims=True)
        grad_query = None
        for i in range(OWN_BLK):
            grad_score = (weights[i] * (pulls[i] - total)).astype(BF16)
            part = dot(grad_score, keys[i])
            grad_query = part if grad_query is None else grad_query + part
            spot = pl.ds(starts[i], BLK)
            sums[spot, :size] += outer_sum(grad_score, queries) * scale
            sums[spot, size:] += outer_sum(weights[i].astype(BF16), grads)
        for i in range(heads):
            out_ref[pl.ds(starts[0], BLK), i * size : (i + 1) * size] = (
                grad_query[i * BLK : (i + 1) * BLK] * scale
            ).astype(BF16)
        return carry

    lax.fori_loop(0, table.shape[1], step, 0)
    out_ref[:, heads * size :] = sums[...].astype(BF16)


def attend(table, rows, heads, size):
    return pl.pallas_call(
        functools.partial(forward_kernel, heads, size),
        out_shape=jax.ShapeDtypeStruct((rows.shape[0], heads * size), BF16),
        in_specs=[
            pl.BlockSpec(memory_space=pltpu.SMEM),
            pl.BlockSpec(memory_space=pltpu.VMEM),
        ],
        out_specs=pl.BlockSpec(memory_space=pltpu.VMEM),
        name="attend",
    )(table, rows)


def attend_back(table, rows, grads, heads, size):
    return pl.pallas_call(
        functools.partial(backward_kernel, heads, size),
        out_shape=jax.ShapeDtypeStruct(rows.shape, BF16),
        in_specs=[
            pl.BlockSpec(memory_space=pltpu.SMEM),
            pl.BlockSpec(memory_space=pltpu.VMEM),
            pl.BlockSpec(memory_space=pltpu.VMEM),
        ],
        out_specs=pl.BlockSpec(memory_space=pltpu.VMEM),
        scratch_shapes=[pltpu.VMEM((rows.shape[0], 2 * size), F32)],
        name="attend_back",
    )(table, rows, grads)


def body(
    tokens,
    out_grad,
    attn_norm,
    w_query,
    key_weight,
    value_weight,
    query_norm,
    key_norm_gain,
    w_out,
    mlp_norm,
    w_gate,
    w_up,
    w_down,
    doc_blocks,
    doc_tail,
    doc_order,
    block_home,
):
    wide_count = lax.axis_size("wide")
    my_wide = lax.axis_index("wide")
    me = lax.axis_index("narrow")
    device_count = wide_count * NARROW
    ring = Ring(wide_count)
    rows = tokens.shape[0]
    block_count = rows // BLK
    head_size = query_norm.shape[0] * device_count
    query_width = w_query.shape[1] // NARROW
    key_width = key_weight.shape[1] // NARROW
    value_heads = key_width // head_size
    group_heads = query_width // key_width
    hidden = w_gate.shape[1] // NARROW
    shard = w_query.shape[0]
    model_width = w_query.shape[1]
    parts = wide_count // (NARROW * value_heads)
    head_width = (group_heads + 2) * head_size

    def narrow_columns(weight):
        return weight.reshape(shard, NARROW, -1).transpose(1, 0, 2)

    def hidden_columns(weight):
        return (
            weight.reshape(shard, wide_count, NARROW, -1)
            .transpose(2, 0, 1, 3)
            .reshape(NARROW, shard, hidden)
        )

    def pad_rows(values):
        return jnp.concatenate([values, jnp.zeros((shard - values.shape[0],), BF16)])

    gains = jnp.stack(
        [attn_norm, mlp_norm, pad_rows(query_norm), pad_rows(key_norm_gain)], axis=1
    )
    gains = jnp.concatenate([gains, jnp.zeros((shard, LANES - 4), BF16)], axis=1)
    first_pieces = jnp.concatenate(
        [
            narrow_columns(w_query),
            narrow_columns(key_weight),
            narrow_columns(value_weight),
            jnp.broadcast_to(gains[None], (NARROW, shard, LANES)),
        ],
        axis=2,
    )
    first_slice = lax.all_to_all(
        first_pieces, "narrow", split_axis=0, concat_axis=0, tiled=True
    ).reshape(NARROW * shard, -1)
    first_full = ring_gather(ring, first_slice)
    projection_width = query_width + 2 * key_width
    projection = first_full[:, :projection_width]
    gain_columns = first_full[:, projection_width : projection_width + 4].astype(F32)
    attention_gain = gain_columns[:, 0]
    mlp_gain = gain_columns[:, 1]
    norm_gains = gain_columns.reshape(device_count, shard, 4)[:, : query_norm.shape[0]]
    query_gain = norm_gains[:, :, 2].reshape(head_size)
    key_gain = norm_gains[:, :, 3].reshape(head_size)

    out_moves = [
        (g, (g % wide_count) * NARROW + g // wide_count) for g in range(device_count)
    ]
    out_weight = ring_gather(ring, lax.ppermute(w_out, DEVICES, out_moves))
    gate_up_pieces = jnp.concatenate([hidden_columns(w_gate), hidden_columns(w_up)], axis=2)
    gate_up = ring_gather(
        ring,
        lax.all_to_all(
            gate_up_pieces, "narrow", split_axis=0, concat_axis=0, tiled=True
        ).reshape(NARROW * shard, -1),
    )
    down = ring_gather(ring, w_down)

    inputs = tokens.astype(F32)
    all_inputs = narrow_gather(tokens).astype(F32)
    normed = row_normalize(all_inputs, attention_gain).astype(BF16)
    raw = dot(normed, projection)
    query_raw = raw[:, :query_width]
    key_raw = raw[:, query_width : query_width + key_width]
    value_rows = raw[:, query_width + key_width :].astype(BF16)
    owner_start, offsets = layout(doc_blocks, doc_order, block_home, my_wide, block_count)
    block_order = me ^ jnp.arange(NARROW, dtype=jnp.int32)
    my_offsets = jnp.take(offsets, block_order, axis=0)
    position = (
        my_offsets.reshape(-1, 1) * BLK + jnp.arange(BLK, dtype=jnp.int32)[None, :]
    ).reshape(-1)
    half_size = head_size // 2
    frequency = THETA ** (-2.0 * jnp.arange(half_size, dtype=F32) / head_size)
    angles = position.astype(F32)[:, None] * frequency[None, :]
    cosines, sines = jnp.cos(angles), jnp.sin(angles)
    cosines = jnp.concatenate([cosines, cosines], axis=-1)
    sines = jnp.concatenate([sines, sines], axis=-1)
    query_rows, query_pull = jax.vjp(
        lambda value, gain: finish_heads(value, gain, cosines, sines), query_raw, query_gain
    )
    key_rows, key_pull = jax.vjp(
        lambda value, gain: finish_heads(value, gain, cosines, sines), key_raw, key_gain
    )

    def by_group(values):
        return jnp.take(values.reshape(NARROW, rows, -1), block_order, axis=0)

    def to_heads(values, per_head):
        values = by_group(values).reshape(NARROW, rows, value_heads, per_head)
        return values.transpose(0, 2, 1, 3)

    def exchange(pieces):
        pieces = jnp.broadcast_to(
            pieces[:, :, None], pieces.shape[:2] + (parts,) + pieces.shape[2:]
        ).reshape(wide_count, rows, -1)
        return lax.all_to_all(pieces, "wide", split_axis=0, concat_axis=0, tiled=True).reshape(
            wide_count * rows, -1
        )

    def exchange_back(values):
        pieces = lax.all_to_all(
            values.reshape(wide_count, rows, -1), "wide", split_axis=0, concat_axis=0, tiled=True
        )
        return pieces.reshape(NARROW, value_heads, parts, rows, -1)[:, :, 0]

    def from_heads(pieces):
        values = pieces.transpose(0, 2, 1, 3).reshape(NARROW, rows, -1)
        return jnp.take(values, block_order, axis=0).reshape(NARROW * rows, -1)

    per_group = group_heads * head_size
    arrived = exchange(
        jnp.concatenate(
            [
                to_heads(query_rows.astype(BF16), per_group),
                to_heads(key_rows.astype(BF16), head_size),
                to_heads(value_rows, head_size),
            ],
            axis=3,
        )
    )
    table = stream_table(
        my_wide // (wide_count // NARROW), owner_start, doc_blocks, doc_tail, block_home, block_count
    )
    attended = attend(table, arrived, group_heads, head_size)
    mixed = from_heads(exchange_back(attended))

    middle = inputs + narrow_reduce(dot(mixed, out_weight))
    normed_two = narrow_gather(row_normalize(middle, mlp_gain).astype(BF16))
    gate_sum = dot(normed_two, gate_up[:, :hidden])
    up_sum = dot(normed_two, gate_up[:, hidden:])
    hidden_rows = gated(gate_sum, up_sum).astype(BF16)
    output = (middle + narrow_reduce(dot(hidden_rows, down))).astype(BF16)

    all_out_grad = narrow_gather(out_grad)
    down_share = ring_reduce(ring, outer_sum(hidden_rows, all_out_grad).astype(BF16))
    grad_hidden = times_transpose(all_out_grad, down)
    unused_gated, gated_pull = jax.vjp(gated, gate_sum, up_sum)
    grad_gate, grad_up = gated_pull(grad_hidden)
    gate_up_grad = jnp.concatenate([grad_gate.astype(BF16), grad_up.astype(BF16)], axis=1)
    grad_normed_two = narrow_reduce(times_transpose(gate_up_grad, gate_up))
    gate_up_share = ring_reduce(ring, outer_sum(normed_two, gate_up_grad).astype(BF16))
    unused_norm, second_pull = jax.vjp(lambda value: row_normalize(value, mlp_gain), middle)
    grad_middle = out_grad.astype(F32) + second_pull(grad_normed_two)[0]

    grad_branch = narrow_gather(grad_middle.astype(BF16))
    grad_mixed = times_transpose(grad_branch, out_weight).astype(BF16)
    arrived_grad = exchange(to_heads(grad_mixed, per_group))
    out_share = ring_reduce(ring, outer_sum(mixed, grad_branch).astype(BF16))
    grad_pieces = exchange_back(
        attend_back(table, arrived, arrived_grad, group_heads, head_size)
    )
    grad_queries = from_heads(grad_pieces[..., :per_group])
    grad_keys = from_heads(grad_pieces[..., per_group : per_group + head_size])
    grad_values = from_heads(grad_pieces[..., per_group + head_size :])
    grad_query_raw, grad_query_gain = query_pull(grad_queries.astype(F32))
    grad_key_raw, grad_key_gain = key_pull(grad_keys.astype(F32))
    projection_grad = jnp.concatenate(
        [grad_query_raw.astype(BF16), grad_key_raw.astype(BF16), grad_values], axis=1
    )
    first_share = ring_reduce(ring, outer_sum(normed, projection_grad).astype(BF16))
    grad_normed = narrow_reduce(times_transpose(projection_grad, projection))
    unused_first, first_pull = jax.vjp(lambda value: row_normalize(value, attention_gain), inputs)
    tokens_grad = (grad_middle + first_pull(grad_normed)[0]).astype(BF16)

    def narrow_rows(share):
        pieces = share.astype(BF16).reshape(NARROW, shard, -1)
        return lax.all_to_all(pieces, "narrow", split_axis=0, concat_axis=0, tiled=True).astype(F32)

    def all_columns(pieces):
        return pieces.transpose(1, 0, 2).reshape(shard, -1)

    def all_hidden(pieces):
        return (
            pieces.reshape(NARROW, shard, wide_count, -1)
            .transpose(1, 2, 0, 3)
            .reshape(shard, NARROW * hidden)
        )

    first_rows = narrow_rows(first_share)
    w_query_grad = all_columns(first_rows[:, :, :query_width])
    w_key_grad = all_columns(first_rows[:, :, query_width : query_width + key_width])
    w_value_grad = all_columns(first_rows[:, :, query_width + key_width :])
    gate_up_rows = narrow_rows(gate_up_share)
    w_gate_grad = all_hidden(gate_up_rows[:, :, :hidden])
    w_up_grad = all_hidden(gate_up_rows[:, :, hidden:])
    w_out_grad = lax.ppermute(
        out_share.astype(BF16), DEVICES, [(b, a) for a, b in out_moves]
    ).astype(F32)

    def row_sums(pairs):
        total = 0.0
        for weight, grad in pairs:
            total = total + jnp.sum(weight.astype(F32) * grad, axis=1)
        return total

    attn_norm_grad = row_sums(
        [(w_query, w_query_grad), (key_weight, w_key_grad), (value_weight, w_value_grad)]
    ) / attn_norm.astype(F32)
    mlp_norm_grad = row_sums([(w_gate, w_gate_grad), (w_up, w_up_grad)]) / mlp_norm.astype(F32)
    norm_grads = everyone_sum(jnp.stack([grad_query_gain, grad_key_gain]), wide_count)
    few = query_norm.shape[0]
    mine = lax.dynamic_slice(norm_grads, (0, (my_wide * NARROW + me) * few), (2, few))
    return (
        output,
        tokens_grad,
        attn_norm_grad,
        w_query_grad,
        w_key_grad,
        w_value_grad,
        mine[0],
        mine[1],
        w_out_grad,
        mlp_norm_grad,
        w_gate_grad,
        w_up_grad,
        down_share,
    )


def solution(mesh):
    rows = P(DEVICES, None)
    vector = P(DEVICES)
    in_specs = (
        (rows, rows, vector, rows, rows, rows, vector, vector, rows, vector, rows, rows, rows)
        + (P(),) * 4
    )
    out_specs = (
        (rows, rows, vector, rows, rows, rows, vector, vector, rows, vector, rows, rows, rows)
    )
    return jax.shard_map(body, mesh=mesh, in_specs=in_specs, out_specs=out_specs, check_vma=False)
```

```python
import functools

import jax
import jax.numpy as jnp
import numpy as np
from jax import lax
from jax.experimental import pallas as pl
from jax.experimental.pallas import tpu as pltpu
from jax.sharding import PartitionSpec as P

BLK = 128
OWN_BLK = 4
EPSILON = 1e-06
THETA = 1000000.0
LANES = 128
NARROW = 4
CONTRACT_ROWS = (((0,), (0,)), ((), ()))
CONTRACT_COLS = (((1,), (1,)), ((), ()))
NEGATIVE = -1e30
F32 = jnp.float32
BF16 = jnp.bfloat16
DEVICES = ("wide", "narrow")


def row_normalize(values, gain_row):
    return (
        values * lax.rsqrt(jnp.mean(values * values, axis=-1, keepdims=True) + EPSILON) * gain_row
    )


def gated(gate_sum, up_sum):
    return jax.nn.silu(gate_sum) * up_sum


def dot(left, right):
    return jnp.dot(left, right, preferred_element_type=F32)


def outer_sum(left_rows, right_rows):
    return lax.dot_general(left_rows, right_rows, CONTRACT_ROWS, preferred_element_type=F32)


def times_transpose(left_rows, matrix):
    return lax.dot_general(left_rows, matrix, CONTRACT_COLS, preferred_element_type=F32)


def ring_order(count):
    rows = count // 2
    return [2 * i for i in range(rows)] + [2 * i + 1 for i in reversed(range(rows))]


class Ring:
    def __init__(self, count):
        self.count = count
        order = ring_order(count)
        place = np.zeros(count, np.int32)
        for i, device in enumerate(order):
            place[device] = i
        self.onward = [(order[i], order[(i + 1) % count]) for i in range(count)]
        self.back = [(b, a) for a, b in self.onward]
        self.order = jnp.asarray(np.array(order + order + order, np.int32))
        self.place = jnp.asarray(place)[lax.axis_index("wide")]

    def device(self, shift):
        return self.order[self.place + self.count + shift]

    def send(self, value, forward):
        return lax.ppermute(value, "wide", self.onward if forward else self.back)


def no_op(out_ref):
    pass


def blank(shape, dtype):
    return pl.pallas_call(
        no_op,
        out_shape=jax.ShapeDtypeStruct(shape, dtype),
        out_specs=pl.BlockSpec(memory_space=pl.ANY),
    )()


def tie(value, *after):
    after = [leaf for leaf in jax.tree.leaves(after)]
    return lax.optimization_barrier((value, after))[0] if after else value


class Gather:
    def __init__(self, ring, part, later=False):
        self.ring, self.rows, self.step, self.later = ring, part.shape[0], 0, later
        self.ahead, self.behind, self.kept = part, part, []
        if ring.count > 8:
            self.whole = lax.all_gather(part, "wide", axis=0, tiled=True)
        else:
            self.whole = blank((ring.count * self.rows, part.shape[1]), part.dtype)
            self.put(part, 0, 0)

    def put(self, value, shift, extra):
        if self.later:
            self.kept.append((value, shift, extra))
        else:
            start = self.ring.device(shift) * self.rows + extra
            self.whole = lax.dynamic_update_slice(self.whole, value, (start, 0))

    def assemble(self, *after):
        if self.ring.count <= 8:
            self.later, kept = False, self.kept
            values = tie([value for value, shift, extra in kept], after)
            for value, (unused_value, shift, extra) in zip(values, kept):
                self.put(value, shift, extra)
        return self.whole

    def advance(self, *after):
        ring, half = self.ring, self.rows // 2
        if ring.count > 8:
            return []
        self.step += 1
        last = self.step == ring.count // 2
        ahead, behind = tie((self.ahead, self.behind), after)
        if last:
            ahead, behind = ahead[:half], behind[half:]
        self.ahead, self.behind = ring.send(ahead, True), ring.send(behind, False)
        self.put(self.ahead, -self.step, 0)
        self.put(self.behind, self.step, half if last else 0)
        return [self.ahead, self.behind]


class Reduce:
    def __init__(self, ring, *terms):
        self.ring, self.terms, self.step = ring, terms, 0
        self.rows = sum(term.shape[0] for term in terms) // ring.count
        if ring.count > 8:
            parts = [term.reshape(ring.count, -1, term.shape[1]) for term in terms]
            whole = jnp.concatenate(parts, axis=1).reshape(-1, terms[0].shape[1])
            self.total = lax.psum_scatter(whole, "wide", scatter_dimension=0, tiled=True)

    def term(self, shift):
        parts = []
        for term in self.terms:
            rows = term.shape[0] // self.ring.count
            start = self.ring.device(shift) * rows
            parts.append(lax.dynamic_slice(term, (start, 0), (rows, term.shape[1])))
        return parts[0] if len(parts) == 1 else jnp.concatenate(parts, axis=0)

    def advance(self, *after):
        ring, half = self.ring, self.rows // 2
        if ring.count > 8:
            return []
        shift = ring.count // 2 - self.step
        if self.step:
            ahead, behind = tie((self.ahead, self.behind), after)
            mine, other = self.term(shift), self.term(-shift)
            if self.step == 1:
                ahead = jnp.concatenate([join(mine[:half], ahead), mine[half:]], axis=0)
                behind = jnp.concatenate([other[:half], join(other[half:], behind)], axis=0)
            else:
                ahead, behind = join(mine, ahead), join(other, behind)
        else:
            far = tie(self.term(shift), after)
            ahead, behind = far[:half], far[half:]
        self.step += 1
        self.ahead, self.behind = ring.send(ahead, True), ring.send(behind, False)
        return [self.ahead, self.behind]

    def result(self):
        if self.ring.count > 8:
            return self.total.astype(F32)
        return self.term(0).astype(F32) + self.ahead.astype(F32) + self.behind.astype(F32)


def join(left, right):
    return (left.astype(F32) + right.astype(F32)).astype(BF16)


def swap(value, bit):
    return lax.ppermute(value, "narrow", [(i, i ^ bit) for i in range(NARROW)])


def narrow_gather(value, across=None):
    across = swap(value, 2) if across is None else across
    chips = jnp.concatenate([value, across], axis=0)
    return jnp.concatenate([chips, swap(chips, 1)], axis=0), across


def narrow_reduce(terms):
    rows = terms.shape[0] // NARROW
    low = terms.astype(BF16)
    other = swap(low[2 * rows :], 1)
    across = swap(join(low[rows : 2 * rows], other[rows:]), 2)
    total = low[:rows].astype(F32) + other[:rows].astype(F32) + across.astype(F32)
    return total, other, across


def layout(doc_blocks, doc_order, block_home, my_wide, block_count):
    owners = doc_blocks.shape[1]
    owner_ids = jnp.arange(owners, dtype=jnp.int32)
    hits = (doc_order[:, :, None] == owner_ids[None, None, :]).astype(jnp.int32)
    in_stream = jnp.sum(hits * doc_blocks[:, None, :], axis=2)
    before = (owner_ids[:, None] < owner_ids[None, :]).astype(jnp.int32)
    stream_start = jnp.sum(in_stream[:, :, None] * before[None], axis=1)
    owner_start = jnp.sum(hits * stream_start[:, :, None], axis=1)
    column = jnp.sum(jnp.where(block_home == my_wide, owner_ids[None, :], 0), axis=1)
    stream_ids = jnp.arange(block_count, dtype=jnp.int32)[None, :] * owners + column[:, None]
    member = (owner_start[:, None, :] <= stream_ids[:, :, None]) & (
        stream_ids[:, :, None] < (owner_start + doc_blocks)[:, None, :]
    )
    offsets = stream_ids - jnp.sum(jnp.where(member, owner_start[:, None, :], 0), axis=2)
    return owner_start, offsets


def stream_table(group, owner_start, doc_blocks, doc_tail, block_home, block_count):
    def pick(table):
        return lax.dynamic_index_in_dim(table, group, 0, keepdims=False)

    starts, blocks, tails, homes = pick(owner_start), pick(doc_blocks), pick(doc_tail), pick(block_home)
    owners = starts.shape[0]
    ids = jnp.arange(owners * block_count, dtype=jnp.int32)
    member = (starts[None, :] <= ids[:, None]) & (ids[:, None] < (starts + blocks)[None, :])

    def chosen(values):
        return jnp.sum(jnp.where(member, values[None, :], 0), axis=1)

    home = jnp.sum(
        jnp.where(
            (ids % owners)[:, None] == jnp.arange(owners, dtype=jnp.int32)[None, :],
            homes[None, :],
            0,
        ),
        axis=1,
    )
    place = home * block_count + ids // owners
    return jnp.stack([place, chosen(starts), chosen((blocks - 1) * BLK + tails)])


def window(table, rows_ref, b, heads, size):
    first, length = table[1, b], table[2, b]
    width = heads * size
    mine = rows_ref[pl.ds(pl.multiple_of(table[0, b] * BLK, BLK), BLK), :width]
    queries = jnp.concatenate([mine[:, i * size : (i + 1) * size] for i in range(heads)], axis=0)
    spot = (b - first) * BLK
    row = lax.broadcasted_iota(jnp.int32, (heads, BLK, BLK), 1).reshape(heads * BLK, BLK) + spot
    col = lax.broadcasted_iota(jnp.int32, (heads * BLK, BLK), 1) + spot
    starts, keys, values, scores = [], [], [], []
    for i in range(OWN_BLK):
        start = pl.multiple_of(table[0, jnp.maximum(b - i, 0)] * BLK, BLK)
        key = rows_ref[pl.ds(start, BLK), width : width + size]
        col_i = col - i * BLK
        allowed = (col_i <= row) & (col_i < length) & (col_i >= 0)
        score = times_transpose(queries, key) * size ** (-0.5)
        starts.append(start)
        keys.append(key)
        values.append(rows_ref[pl.ds(start, BLK), width + size : width + 2 * size])
        scores.append(jnp.where(allowed, score, NEGATIVE))
    highest = scores[0]
    for score in scores[1:]:
        highest = jnp.maximum(highest, score)
    highest = jnp.max(highest, axis=-1, keepdims=True)
    powers = [jnp.exp(score - highest) for score in scores]
    total = powers[0]
    for power in powers[1:]:
        total = total + power
    total = jnp.sum(total, axis=-1, keepdims=True)
    weights = [power / total for power in powers]
    return mine, queries, starts, keys, values, weights


def forward_kernel(heads, size, table, rows_ref, out_ref):
    def step(b, carry):
        _, _, starts, _, values, weights = window(table, rows_ref, b, heads, size)
        mixed = dot(weights[0].astype(BF16), values[0])
        for weight, value in zip(weights[1:], values[1:]):
            mixed = mixed + dot(weight.astype(BF16), value)
        for i in range(heads):
            out_ref[pl.ds(starts[0], BLK), i * size : (i + 1) * size] = mixed[
                i * BLK : (i + 1) * BLK
            ].astype(BF16)
        return carry

    lax.fori_loop(0, table.shape[1], step, 0)


def backward_kernel(heads, size, table, rows_ref, grad_ref, out_ref, sums):
    sums[...] = jnp.zeros_like(sums)
    scale = size ** (-0.5)

    def step(b, carry):
        _, queries, starts, keys, values, weights = window(table, rows_ref, b, heads, size)
        grads = grad_ref[pl.ds(starts[0], BLK), :]
        grads = jnp.concatenate([grads[:, i * size : (i + 1) * size] for i in range(heads)], axis=0)
        pulls = [times_transpose(grads, value) for value in values]
        total = weights[0] * pulls[0]
        for weight, pull in zip(weights[1:], pulls[1:]):
            total = total + weight * pull
        total = jnp.sum(total, axis=-1, keepdims=True)
        grad_query = None
        for i in range(OWN_BLK):
            grad_score = (weights[i] * (pulls[i] - total)).astype(BF16)
            part = dot(grad_score, keys[i])
            grad_query = part if grad_query is None else grad_query + part
            spot = pl.ds(starts[i], BLK)
            sums[spot, :size] += outer_sum(grad_score, queries) * scale
            sums[spot, size:] += outer_sum(weights[i].astype(BF16), grads)
        for i in range(heads):
            out_ref[pl.ds(starts[0], BLK), i * size : (i + 1) * size] = (
                grad_query[i * BLK : (i + 1) * BLK] * scale
            ).astype(BF16)
        return carry

    lax.fori_loop(0, table.shape[1], step, 0)
    out_ref[:, heads * size :] = sums[...].astype(BF16)


def attend(table, rows, heads, size):
    return pl.pallas_call(
        functools.partial(forward_kernel, heads, size),
        out_shape=jax.ShapeDtypeStruct((rows.shape[0], heads * size), BF16),
        in_specs=[
            pl.BlockSpec(memory_space=pltpu.SMEM),
            pl.BlockSpec(memory_space=pltpu.VMEM),
        ],
        out_specs=pl.BlockSpec(memory_space=pltpu.VMEM),
        name="attend",
    )(table, rows)


def attend_back(table, rows, grads, heads, size):
    return pl.pallas_call(
        functools.partial(backward_kernel, heads, size),
        out_shape=jax.ShapeDtypeStruct(rows.shape, BF16),
        in_specs=[
            pl.BlockSpec(memory_space=pltpu.SMEM),
            pl.BlockSpec(memory_space=pltpu.VMEM),
            pl.BlockSpec(memory_space=pltpu.VMEM),
        ],
        out_specs=pl.BlockSpec(memory_space=pltpu.VMEM),
        scratch_shapes=[pltpu.VMEM((rows.shape[0], 2 * size), F32)],
        name="attend_back",
    )(table, rows, grads)


def unit_rows(values):
    return lax.rsqrt(jnp.mean(values * values, axis=-1, keepdims=True) + EPSILON)


def finish_kernel(sizes, order, raw_ref, cos_ref, sin_ref, gains_ref, out_ref):
    value_heads, group_heads, size = sizes
    per_group = group_heads * size
    query_width = value_heads * per_group
    key_width = value_heads * size

    def turned(start, gain):
        values = raw_ref[:, start : start + size]
        values = values * unit_rows(values) * gain
        return (
            values * cos_ref[...] + pltpu.roll(values, size // 2, 1) * sin_ref[...]
        ).astype(BF16)

    for head in range(value_heads):
        for i in range(group_heads):
            start = head * per_group + i * size
            out_ref[0, head, :, i * size : (i + 1) * size] = turned(start, gains_ref[0:1, :])
        start = query_width + head * size
        out_ref[0, head, :, per_group : per_group + size] = turned(start, gains_ref[1:2, :])
        start = query_width + key_width + head * size
        out_ref[0, head, :, per_group + size :] = raw_ref[:, start : start + size].astype(BF16)


def unfinish_kernel(
    sizes, order, raw_ref, grad_ref, cos_ref, sin_ref, gains_ref, out_ref, sums_ref
):
    value_heads, group_heads, size = sizes
    per_group = group_heads * size
    query_width = value_heads * per_group
    key_width = value_heads * size

    @pl.when(pl.program_id(0) == 0)
    def _():
        sums_ref[...] = jnp.zeros_like(sums_ref)

    def pull(grad, start, which):
        grad = grad.astype(F32)
        values = raw_ref[:, start : start + size]
        unit = unit_rows(values)
        values = values * unit
        grad = grad * cos_ref[...] + pltpu.roll(grad * sin_ref[...], size // 2, 1)
        sums_ref[which * 8 : which * 8 + 8, :] += jnp.sum(
            (grad * values).reshape(-1, 8, size), axis=0
        )
        grad = grad * gains_ref[which : which + 1, :]
        grad = unit * (grad - values * jnp.mean(grad * values, axis=-1, keepdims=True))
        out_ref[:, start : start + size] = grad.astype(BF16)

    for head in range(value_heads):
        for i in range(group_heads):
            pull(
                grad_ref[0, head, :, i * size : (i + 1) * size], head * per_group + i * size, 0
            )
        pull(grad_ref[0, head, :, per_group : per_group + size], query_width + head * size, 1)
        start = query_width + key_width + head * size
        out_ref[:, start : start + size] = grad_ref[0, head, :, per_group + size :]


def pack_kernel(heads, order, rows_ref, out_ref):
    width = out_ref.shape[3]
    for head in range(heads):
        out_ref[0, head] = rows_ref[:, head * width : (head + 1) * width]


def unpack_kernel(heads, order, pieces_ref, out_ref):
    width = pieces_ref.shape[3]
    for head in range(heads):
        out_ref[:, head * width : (head + 1) * width] = pieces_ref[0, head]


def row_spec(rows, cols):
    return pl.BlockSpec((rows, cols), lambda i, order: (i, 0))


def whole_spec(shape):
    return pl.BlockSpec(shape, lambda i, order: (0,) * len(shape))


def piece_spec(heads, rows, cols):
    return pl.BlockSpec((1, heads, rows, cols), lambda i, order: (order[i], 0, 0, 0))


def by_rows(kernel, name, order, args, in_specs, out_shape, out_specs, cost):
    return pl.pallas_call(
        kernel,
        grid_spec=pltpu.PrefetchScalarGridSpec(
            num_scalar_prefetch=1, grid=(NARROW,), in_specs=in_specs, out_specs=out_specs
        ),
        out_shape=out_shape,
        cost_estimate=pl.CostEstimate(flops=cost, bytes_accessed=cost, transcendentals=0),
        name=name,
    )(order, *args)


def finish(sizes, order, raw, cosines, sines, gains):
    value_heads, group_heads, size = sizes
    rows = raw.shape[0] // NARROW
    width = (group_heads + 2) * size
    return by_rows(
        functools.partial(finish_kernel, sizes),
        "finish",
        order,
        (raw, cosines, sines, gains),
        [
            row_spec(rows, raw.shape[1]),
            row_spec(rows, size),
            row_spec(rows, size),
            whole_spec(gains.shape),
        ],
        jax.ShapeDtypeStruct((NARROW, value_heads, rows, width), BF16),
        piece_spec(value_heads, rows, width),
        8 << 20,
    )


def unfinish(sizes, order, raw, pieces, cosines, sines, gains):
    value_heads, group_heads, size = sizes
    rows = raw.shape[0] // NARROW
    return by_rows(
        functools.partial(unfinish_kernel, sizes),
        "unfinish",
        order,
        (raw, pieces, cosines, sines, gains),
        [
            row_spec(rows, raw.shape[1]),
            piece_spec(value_heads, rows, pieces.shape[3]),
            row_spec(rows, size),
            row_spec(rows, size),
            whole_spec(gains.shape),
        ],
        (
            jax.ShapeDtypeStruct(raw.shape, BF16),
            jax.ShapeDtypeStruct((16, size), F32),
        ),
        (row_spec(rows, raw.shape[1]), whole_spec((16, size))),
        8 << 20,
    )


def pack(heads, order, values):
    rows = values.shape[0] // NARROW
    width = values.shape[1] // heads
    return by_rows(
        functools.partial(pack_kernel, heads),
        "pack",
        order,
        (values,),
        [row_spec(rows, values.shape[1])],
        jax.ShapeDtypeStruct((NARROW, heads, rows, width), BF16),
        piece_spec(heads, rows, width),
        2 << 20,
    )


def unpack(order, pieces):
    heads, rows, width = pieces.shape[1:]
    return by_rows(
        functools.partial(unpack_kernel, heads),
        "unpack",
        order,
        (pieces,),
        [piece_spec(heads, rows, width)],
        jax.ShapeDtypeStruct((NARROW * rows, heads * width), BF16),
        row_spec(rows, heads * width),
        2 << 20,
    )


def split_kernel(block, gate_ref, up_ref, out_ref):
    places = gate_ref.shape[1] // (block * NARROW)
    half = out_ref.shape[2] // 2
    for i, ref in enumerate((gate_ref, up_ref)):
        for n in range(NARROW):
            for place in range(places):
                chunk, spot = divmod(place, places // 2)
                start = chunk * half + i * (half // 2) + spot * block
                source = (place * NARROW + n) * block
                out_ref[n, :, start : start + block] = ref[:, source : source + block]


def merge_kernel(block, first_ref, second_ref, gate_ref, up_ref):
    places = gate_ref.shape[1] // (block * NARROW)
    half = first_ref.shape[2]
    for i, ref in enumerate((gate_ref, up_ref)):
        for n in range(NARROW):
            for place in range(places):
                chunk, spot = divmod(place, places // 2)
                source = (first_ref, second_ref)[chunk]
                start = i * (half // 2) + spot * block
                target = (place * NARROW + n) * block
                ref[:, target : target + block] = source[n, :, start : start + block].astype(F32)


def split_columns(block, gate, up):
    rows, cols = gate.shape
    if block % 64:
        def by_chunk(values):
            values = values.reshape(rows, 2, -1, NARROW, block).transpose(3, 0, 1, 2, 4)
            return values.reshape(NARROW, rows, 2, -1)

        both = jnp.concatenate([by_chunk(gate), by_chunk(up)], axis=3)
        return both.reshape(NARROW, rows, -1)
    return pl.pallas_call(
        functools.partial(split_kernel, block),
        out_shape=jax.ShapeDtypeStruct((NARROW, rows, 2 * cols // NARROW), BF16),
        name="split_columns",
    )(gate, up)


def merge_columns(block, first, second):
    rows, half = first.shape[1:]
    cols = half * NARROW
    if block % 64:
        both = jnp.stack([first, second], axis=2).reshape(NARROW, rows, 2, 2, -1, block)
        both = both.transpose(3, 1, 2, 4, 0, 5).reshape(2, rows, cols).astype(F32)
        return both[0], both[1]
    return pl.pallas_call(
        functools.partial(merge_kernel, block),
        out_shape=(jax.ShapeDtypeStruct((rows, cols), F32),) * 2,
        name="merge_columns",
    )(first, second)


def body(
    tokens,
    out_grad,
    attn_norm,
    w_query,
    key_weight,
    value_weight,
    query_norm,
    key_norm_gain,
    w_out,
    mlp_norm,
    w_gate,
    w_up,
    w_down,
    doc_blocks,
    doc_tail,
    doc_order,
    block_home,
):
    wide_count = lax.axis_size("wide")
    my_wide = lax.axis_index("wide")
    me = lax.axis_index("narrow")
    device_count = wide_count * NARROW
    ring = Ring(wide_count)
    rows = tokens.shape[0]
    block_count = rows // BLK
    head_size = query_norm.shape[0] * device_count
    query_width = w_query.shape[1] // NARROW
    key_width = key_weight.shape[1] // NARROW
    value_heads = key_width // head_size
    group_heads = query_width // key_width
    hidden = w_gate.shape[1] // NARROW
    shard = w_query.shape[0]
    parts = wide_count // (NARROW * value_heads)

    order = me ^ jnp.array([0, 2, 1, 3], dtype=jnp.int32)
    partner = me ^ jnp.arange(NARROW, dtype=jnp.int32)
    sizes = (value_heads, group_heads, head_size)

    def narrow_exchange(pieces):
        pieces = jnp.take(pieces, partner, axis=0)
        moved = [pieces[0]] + [swap(pieces[i], i) for i in range(1, NARROW)]
        return jnp.take(jnp.stack(moved), partner, axis=0)

    def narrow_columns(weight):
        return weight.reshape(shard, NARROW, -1).transpose(1, 0, 2)

    def pad_lanes(values, size):
        return jnp.concatenate([values, jnp.zeros((size - values.shape[0],), BF16)])

    projection_width = query_width + 2 * key_width
    gains = [pad_lanes(gain, shard) for gain in (attn_norm, mlp_norm, query_norm, key_norm_gain)]
    gains = pad_lanes(jnp.concatenate(gains), projection_width)[None, :]
    extra = 32
    at_row = lax.broadcasted_iota(jnp.int32, (extra, projection_width), 0) == me
    gain_rows = jnp.broadcast_to(jnp.where(at_row, gains, 0)[None], (NARROW, extra, projection_width))
    first_pieces = jnp.concatenate(
        [narrow_columns(w_query), narrow_columns(key_weight), narrow_columns(value_weight)], axis=2
    )
    first_pieces = narrow_exchange(jnp.concatenate([first_pieces, gain_rows], axis=1))
    tokens_across = swap(tokens, 2)
    moves = [(g, (g % wide_count) * NARROW + g // wide_count) for g in range(device_count)]
    moves_back = [(b, a) for a, b in moves]
    out_part = lax.ppermute(w_out, DEVICES, moves)
    folds = w_out.shape[1] // projection_width
    out_part = out_part.reshape(shard, folds, -1).transpose(1, 0, 2).reshape(folds * shard, -1)
    gain_rows = jnp.sum(first_pieces[:, shard:].astype(F32), axis=0).astype(BF16)
    first_part = jnp.concatenate(
        [first_pieces[:, :shard].reshape(NARROW * shard, -1), out_part, gain_rows], axis=0
    )
    block = w_down.shape[0]
    first_ring = Gather(ring, first_part)
    down_ring = Gather(ring, w_down, later=True)
    begun = first_ring.advance(down_ring.advance())
    first_ring.advance()
    gate_part, up_part = tie((w_gate, w_up), begun)
    gate_up_pieces = split_columns(block, gate_part, up_part)
    gate_up_part = narrow_exchange(gate_up_pieces).reshape(NARROW * shard, -1)
    first_ring.advance(tokens_across)
    first_done = first_ring.advance()
    gathered = first_ring.whole.reshape(wide_count, -1, projection_width)
    projection = gathered[:, : NARROW * shard].reshape(-1, projection_width)
    out_rows = gathered[:, NARROW * shard : (NARROW + folds) * shard]
    out_rows = out_rows.reshape(wide_count, folds, shard, -1).transpose(0, 2, 1, 3)
    out_weight = out_rows.reshape(wide_count * shard, -1)
    gain_rows = gathered[:, (NARROW + folds) * shard :][:, :NARROW, : 4 * shard]
    gain_rows = gain_rows.reshape(device_count, 4, shard).astype(F32)
    attention_gain, mlp_gain = gain_rows[:, 0].reshape(-1), gain_rows[:, 1].reshape(-1)
    few = query_norm.shape[0]
    norm_gains = jnp.stack(
        [gain_rows[:, 2, :few].reshape(head_size), gain_rows[:, 3, :few].reshape(head_size)]
    )
    norm_gains = jnp.concatenate([norm_gains, jnp.zeros((6, head_size), F32)])
    rings = [
        Gather(ring, gate_up_part[:, :hidden], later=True),
        Gather(ring, gate_up_part[:, hidden:]),
    ]

    inputs = tokens.astype(F32)
    all_inputs = narrow_gather(tokens, tokens_across)[0].astype(F32)
    normed = row_normalize(all_inputs, attention_gain).astype(BF16)
    raw = dot(normed, projection)
    owner_start, offsets = layout(
        doc_blocks, doc_order, tie(block_home, begun), my_wide, block_count
    )
    my_offsets = jnp.take(offsets, order, axis=0)
    position = (
        my_offsets.reshape(-1, 1) * BLK + jnp.arange(BLK, dtype=jnp.int32)[None, :]
    ).reshape(-1)
    half_size = head_size // 2
    frequency = THETA ** (-2.0 * jnp.arange(half_size, dtype=F32) / head_size)
    angles = position.astype(F32)[:, None] * frequency[None, :]
    cosines, sines = jnp.cos(angles), jnp.sin(angles)
    cosines = jnp.concatenate([cosines, cosines], axis=-1)
    sines = jnp.concatenate([-sines, sines], axis=-1)

    def exchange(pieces):
        pieces = jnp.broadcast_to(
            pieces[:, :, None], pieces.shape[:2] + (parts,) + pieces.shape[2:]
        ).reshape(wide_count, rows, -1)
        return lax.all_to_all(pieces, "wide", split_axis=0, concat_axis=0, tiled=True).reshape(
            wide_count * rows, -1
        )

    def exchange_back(values):
        pieces = lax.all_to_all(
            values.reshape(wide_count, rows, -1), "wide", split_axis=0, concat_axis=0, tiled=True
        )
        return pieces.reshape(NARROW, value_heads, parts, rows, -1)[:, :, 0]

    finished = finish(sizes, order, raw, cosines, sines, norm_gains)
    arrived = exchange(tie(finished, down_ring.advance(first_done, gate_up_part)))
    table = stream_table(
        my_wide // (wide_count // NARROW), owner_start, doc_blocks, doc_tail, block_home, block_count
    )
    all_out_grad, unused_across = narrow_gather(tie(out_grad, finished))
    arrived = tie(arrived, rings[0].advance(finished), all_out_grad)
    attended = tie(attend(table, arrived, group_heads, head_size), rings[0].advance(arrived))
    mixed = tie(exchange_back(attended), down_ring.advance(attended))
    early = rings[0].advance(mixed)
    mixed = unpack(order, mixed)

    reduced, unused_other, across = narrow_reduce(dot(mixed, out_weight))
    middle = inputs + tie(reduced, early)
    normed_rows = row_normalize(middle, mlp_gain).astype(BF16)
    early = [rings[0].advance(normed_rows), rings[1].advance(normed_rows)]
    across = tie(swap(normed_rows, 2), early)
    late = down_ring.advance(normed_rows)
    normed_two, across = narrow_gather(normed_rows, across)
    normed_two = tie(normed_two, late)
    gate_up_first, down = rings[0].assemble(middle), down_ring.assemble(middle)
    part = hidden // 2

    def half_forward(rows, weights):
        gate_sum, up_sum = dot(rows, weights[:, :part]), dot(rows, weights[:, part:])
        return gate_sum, up_sum, gated(gate_sum, up_sum).astype(BF16)

    def half_back(gate_sum, up_sum, grad_hidden):
        unused_gated, pull = jax.vjp(gated, gate_sum, up_sum)
        return jnp.concatenate([grad.astype(BF16) for grad in pull(grad_hidden)], axis=1)

    early = rings[1].advance(normed_two)
    gate_sum, up_sum, hidden_first = half_forward(normed_two, gate_up_first)
    wait_first = tie(all_out_grad, hidden_first, early)
    early = rings[1].advance(hidden_first)
    grad_first = half_back(gate_sum, up_sum, times_transpose(wait_first, down[:part]))
    grad_first = tie(grad_first, early)
    early = rings[1].advance(grad_first)
    first_half_terms = outer_sum(normed_two, grad_first).astype(BF16)
    first_half = Reduce(ring, first_half_terms)
    grad_terms = times_transpose(tie(grad_first, first_half_terms, early), gate_up_first)
    grad_terms = tie(grad_terms, first_half.advance())
    early = first_half.advance(grad_terms)
    gate_sum, up_sum, hidden_second = half_forward(tie(normed_two, grad_terms), rings[1].whole)
    wait_second = tie(all_out_grad, hidden_second, early)
    early = first_half.advance(hidden_second)
    grad_second = half_back(gate_sum, up_sum, times_transpose(wait_second, down[part:]))
    grad_second = tie(grad_second, early)
    early = first_half.advance(grad_second)
    grad_terms = (grad_terms + times_transpose(grad_second, rings[1].whole)).astype(BF16)
    grad_normed_two, other, across = narrow_reduce(tie(grad_terms, early))
    later_grad, later_normed, hidden_rows = tie(
        (grad_second, normed_two, (hidden_first, hidden_second)), other
    )
    hidden_rows = jnp.concatenate(hidden_rows, axis=1)
    down_terms = outer_sum(hidden_rows, all_out_grad).astype(BF16)
    down_sums = Reduce(ring, down_terms)
    second_half_terms = outer_sum(later_normed, tie(later_grad, down_terms)).astype(BF16)
    second_half = Reduce(ring, second_half_terms)
    early = [down_sums.advance(), second_half.advance()]
    grad_normed_two = tie(grad_normed_two, early)
    unused_norm, second_pull = jax.vjp(lambda value: row_normalize(value, mlp_gain), middle)
    grad_middle = out_grad.astype(F32) + second_pull(grad_normed_two)[0]

    branch_rows = grad_middle.astype(BF16)
    early = second_half.advance(branch_rows)
    late = down_sums.advance(branch_rows)
    across = tie(swap(branch_rows, 2), early)
    grad_branch, across = narrow_gather(branch_rows, across)
    grad_branch = tie(grad_branch, late)
    early = [second_half.advance(grad_branch), down_sums.advance(grad_branch)]
    grad_mixed = times_transpose(grad_branch, out_weight).astype(BF16)
    grad_pack = pack(value_heads, order, grad_mixed)
    later_hidden = tie(hidden_rows, grad_pack)
    arrived_grad = tie(exchange(grad_pack), early)

    def narrow_rows(share):
        return narrow_exchange(share.astype(BF16).reshape(NARROW, shard, -1))

    grad_pieces = attend_back(table, arrived, arrived_grad, group_heads, head_size)
    later_branch = tie(grad_branch, grad_pieces)
    out_terms = outer_sum(mixed, later_branch).astype(BF16)
    early = [second_half.advance(grad_pieces), down_sums.advance(grad_pieces)]
    first_rows = narrow_rows(tie(first_half.result(), arrived_grad))
    output = (middle + narrow_reduce(dot(later_hidden, down))[0]).astype(BF16)
    grad_pieces = tie(exchange_back(grad_pieces), early, first_rows, output, out_terms)
    projection_grad, norm_sums = unfinish(
        sizes, order, raw, grad_pieces, cosines, sines, norm_gains
    )
    first_terms = outer_sum(normed, projection_grad).astype(BF16)
    out_terms = out_terms.reshape(wide_count, shard, folds, -1).transpose(0, 2, 1, 3)
    norm_terms = jnp.sum(norm_sums.reshape(2, 8, head_size), axis=1)
    norm_terms = norm_terms.reshape(2, wide_count, NARROW, few).transpose(1, 2, 0, 3)
    norm_terms = norm_terms.reshape(wide_count, NARROW, 2 * few).astype(BF16)
    norm_terms = jnp.pad(
        norm_terms, ((0, 0), (0, extra - NARROW), (0, projection_width - 2 * few))
    )
    first_sums = Reduce(
        ring,
        first_terms,
        out_terms.reshape(-1, projection_width),
        norm_terms.reshape(-1, projection_width),
    )
    first_sums.advance()
    grad_normed, other, across = narrow_reduce(
        times_transpose(tie(projection_grad, first_terms), projection)
    )
    second = first_sums.advance(other)
    second_rows = narrow_rows(tie(second_half.result(), second))
    first_sums.advance()
    w_gate_grad, w_up_grad = merge_columns(block, first_rows, second_rows)
    first_sums.advance(second_rows, across)
    unused_first, first_pull = jax.vjp(lambda value: row_normalize(value, attention_gain), inputs)
    tokens_grad = (grad_middle + first_pull(grad_normed)[0]).astype(BF16)

    def all_columns(pieces):
        return pieces.astype(F32).transpose(1, 0, 2).reshape(shard, -1)

    share = first_sums.result().astype(BF16)
    out_share = share[NARROW * shard : (NARROW + folds) * shard].reshape(folds, shard, -1)
    out_share = out_share.transpose(1, 0, 2).reshape(shard, -1)
    w_out_grad = lax.ppermute(out_share, DEVICES, moves_back).astype(F32)
    norm_rows = share[(NARROW + folds) * shard :][:NARROW, None, :]
    norm_rows = jnp.pad(norm_rows, ((0, 0), (0, 15), (0, 0)))
    projection_rows = narrow_exchange(
        jnp.concatenate([share[: NARROW * shard].reshape(NARROW, shard, -1), norm_rows], axis=1)
    )
    norm_grads = jnp.sum(projection_rows[:, shard, : 2 * few].astype(F32), axis=0)
    projection_rows = projection_rows[:, :shard]
    w_query_grad = all_columns(projection_rows[:, :, :query_width])
    w_key_grad = all_columns(projection_rows[:, :, query_width : query_width + key_width])
    w_value_grad = all_columns(projection_rows[:, :, query_width + key_width :])
    w_down_grad = down_sums.result()

    def row_sums(pairs):
        total = 0.0
        for weight, grad in pairs:
            total = total + jnp.sum(weight.astype(F32) * grad, axis=1)
        return total

    attn_norm_grad = row_sums(
        [(w_query, w_query_grad), (key_weight, w_key_grad), (value_weight, w_value_grad)]
    ) / attn_norm.astype(F32)
    mlp_norm_grad = row_sums([(w_gate, w_gate_grad), (w_up, w_up_grad)]) / mlp_norm.astype(F32)
    return (
        output,
        tokens_grad,
        attn_norm_grad,
        w_query_grad,
        w_key_grad,
        w_value_grad,
        norm_grads[:few],
        norm_grads[few:],
        w_out_grad,
        mlp_norm_grad,
        w_gate_grad,
        w_up_grad,
        w_down_grad,
    )


def solution(mesh):
    rows = P(DEVICES, None)
    vector = P(DEVICES)
    in_specs = (
        (rows, rows, vector, rows, rows, rows, vector, vector, rows, vector, rows, rows, rows)
        + (P(),) * 4
    )
    out_specs = (
        (rows, rows, vector, rows, rows, rows, vector, vector, rows, vector, rows, rows, rows)
    )
    return jax.shard_map(body, mesh=mesh, in_specs=in_specs, out_specs=out_specs, check_vma=False)
```

```python
import functools

import jax
import jax.numpy as jnp
import numpy as np
from jax import lax
from jax.experimental import pallas as pl
from jax.experimental.pallas import tpu as pltpu
from jax.sharding import PartitionSpec as P

BLK = 128
OWN_BLK = 4
EPSILON = 1e-06
THETA = 1000000.0
LANES = 128
NARROW = 4
CONTRACT_ROWS = (((0,), (0,)), ((), ()))
CONTRACT_COLS = (((1,), (1,)), ((), ()))
NEGATIVE = -1e30
F32 = jnp.float32
BF16 = jnp.bfloat16
DEVICES = ("wide", "narrow")


def row_normalize(values, gain_row):
    return (
        values * lax.rsqrt(jnp.mean(values * values, axis=-1, keepdims=True) + EPSILON) * gain_row
    )


def gated(gate_sum, up_sum):
    return jax.nn.silu(gate_sum) * up_sum


def dot(left, right):
    return jnp.dot(left, right, preferred_element_type=F32)


def outer_sum(left_rows, right_rows):
    return lax.dot_general(left_rows, right_rows, CONTRACT_ROWS, preferred_element_type=F32)


def times_transpose(left_rows, matrix):
    return lax.dot_general(left_rows, matrix, CONTRACT_COLS, preferred_element_type=F32)


def ring_order(count):
    rows = count // 2
    return [2 * i for i in range(rows)] + [2 * i + 1 for i in reversed(range(rows))]


class Ring:
    def __init__(self, count):
        self.count = count
        order = ring_order(count)
        place = np.zeros(count, np.int32)
        for i, device in enumerate(order):
            place[device] = i
        self.onward = [(order[i], order[(i + 1) % count]) for i in range(count)]
        self.back = [(b, a) for a, b in self.onward]
        self.order = jnp.asarray(np.array(order + order + order, np.int32))
        self.place = jnp.asarray(place)[lax.axis_index("wide")]

    def device(self, shift):
        return self.order[self.place + self.count + shift]

    def send(self, value, forward):
        return lax.ppermute(value, "wide", self.onward if forward else self.back)


def no_op(out_ref):
    pass


def blank(shape, dtype):
    return pl.pallas_call(
        no_op,
        out_shape=jax.ShapeDtypeStruct(shape, dtype),
        out_specs=pl.BlockSpec(memory_space=pl.ANY),
    )()


def tie(value, *after):
    after = [leaf for leaf in jax.tree.leaves(after)]
    return lax.optimization_barrier((value, after))[0] if after else value


class Gather:
    def __init__(self, ring, part):
        self.ring, self.rows, self.step, self.flight = ring, part.shape[0], 0, []
        self.ahead, self.behind = part, part
        if ring.count > 8:
            self.whole = lax.all_gather(part, "wide", axis=0, tiled=True)
        else:
            self.whole = self.put(
                blank((ring.count * self.rows, part.shape[1]), part.dtype), part, 0, 0
            )

    def put(self, whole, value, shift, extra):
        return lax.dynamic_update_slice(
            whole, value, (self.ring.device(shift) * self.rows + extra, 0)
        )

    def advance(self, *after):
        ring, half = self.ring, self.rows // 2
        if ring.count > 8:
            return []
        self.step += 1
        last = self.step == ring.count // 2
        ahead, behind = tie((self.ahead, self.behind), after)
        if last:
            ahead, behind = ahead[:half], behind[half:]
        self.ahead, self.behind = ring.send(ahead, True), ring.send(behind, False)
        self.whole = self.put(self.whole, self.ahead, -self.step, 0)
        self.whole = self.put(self.whole, self.behind, self.step, half if last else 0)
        return [self.ahead, self.behind]


class Reduce:
    def __init__(self, ring, *terms, shared=None):
        self.ring, self.terms, self.shared, self.step = ring, terms, shared, 0
        if ring.count > 8:
            parts = [term.reshape(ring.count, -1, term.shape[1]) for term in terms]
            if shared is not None:
                parts.append(jnp.broadcast_to(shared[None], (ring.count,) + shared.shape))
            whole = jnp.concatenate(parts, axis=1).reshape(-1, terms[0].shape[1])
            self.total = lax.psum_scatter(whole, "wide", scatter_dimension=0, tiled=True)

    def term(self, shift):
        parts = []
        for term in self.terms:
            rows = term.shape[0] // self.ring.count
            start = self.ring.device(shift) * rows
            parts.append(lax.dynamic_slice(term, (start, 0), (rows, term.shape[1])))
        if self.shared is not None:
            parts.append(self.shared)
        return parts[0] if len(parts) == 1 else jnp.concatenate(parts, axis=0)

    def advance(self, *after):
        ring = self.ring
        if ring.count > 8:
            return []
        shift = ring.count // 2 - self.step
        if self.step:
            ahead, behind = tie((self.ahead, self.behind), after)
            mine, other = self.term(shift), self.term(-shift)
            half = mine.shape[0] // 2
            if self.step == 1:
                ahead = jnp.concatenate([join(mine[:half], ahead), mine[half:]], axis=0)
                behind = jnp.concatenate([other[:half], join(other[half:], behind)], axis=0)
            else:
                ahead, behind = join(mine, ahead), join(other, behind)
        else:
            far = tie(self.term(shift), after)
            half = far.shape[0] // 2
            ahead, behind = far[:half], far[half:]
        self.step += 1
        self.ahead, self.behind = ring.send(ahead, True), ring.send(behind, False)
        return [self.ahead, self.behind]

    def result(self):
        if self.ring.count > 8:
            return self.total.astype(F32)
        return self.term(0).astype(F32) + self.ahead.astype(F32) + self.behind.astype(F32)


def join(left, right):
    return (left.astype(F32) + right.astype(F32)).astype(BF16)


def swap(value, bit):
    return lax.ppermute(value, "narrow", [(i, i ^ bit) for i in range(NARROW)])


def narrow_gather(value, across=None):
    across = swap(value, 2) if across is None else across
    return jnp.concatenate([value, swap(value, 1), across, swap(across, 1)], axis=0), across


def narrow_reduce(terms):
    rows = terms.shape[0] // NARROW
    low = terms.astype(BF16)
    parts = [low[i * rows : (i + 1) * rows] for i in range(NARROW)]
    near, far = swap(parts[1], 1), swap(parts[3], 1)
    across = swap(join(parts[2], far), 2)
    return parts[0].astype(F32) + near.astype(F32) + across.astype(F32), (near, far), across


def layout(doc_blocks, doc_order, block_home, my_wide, block_count):
    owners = doc_blocks.shape[1]
    owner_ids = jnp.arange(owners, dtype=jnp.int32)
    hits = (doc_order[:, :, None] == owner_ids[None, None, :]).astype(jnp.int32)
    in_stream = jnp.sum(hits * doc_blocks[:, None, :], axis=2)
    before = (owner_ids[:, None] < owner_ids[None, :]).astype(jnp.int32)
    stream_start = jnp.sum(in_stream[:, :, None] * before[None], axis=1)
    owner_start = jnp.sum(hits * stream_start[:, :, None], axis=1)
    column = jnp.sum(jnp.where(block_home == my_wide, owner_ids[None, :], 0), axis=1)
    stream_ids = jnp.arange(block_count, dtype=jnp.int32)[None, :] * owners + column[:, None]
    member = (owner_start[:, None, :] <= stream_ids[:, :, None]) & (
        stream_ids[:, :, None] < (owner_start + doc_blocks)[:, None, :]
    )
    offsets = stream_ids - jnp.sum(jnp.where(member, owner_start[:, None, :], 0), axis=2)
    return owner_start, offsets


def stream_table(group, owner_start, doc_blocks, doc_tail, block_home, block_count):
    def pick(table):
        return lax.dynamic_index_in_dim(table, group, 0, keepdims=False)

    starts, blocks, tails, homes = pick(owner_start), pick(doc_blocks), pick(doc_tail), pick(block_home)
    owners = starts.shape[0]
    ids = jnp.arange(owners * block_count, dtype=jnp.int32)
    member = (starts[None, :] <= ids[:, None]) & (ids[:, None] < (starts + blocks)[None, :])

    def chosen(values):
        return jnp.sum(jnp.where(member, values[None, :], 0), axis=1)

    home = jnp.sum(
        jnp.where(
            (ids % owners)[:, None] == jnp.arange(owners, dtype=jnp.int32)[None, :],
            homes[None, :],
            0,
        ),
        axis=1,
    )
    place = home * block_count + ids // owners
    return jnp.stack([place, chosen(starts), chosen((blocks - 1) * BLK + tails)])


def window(table, rows_ref, b, heads, size):
    first, length = table[1, b], table[2, b]
    width = heads * size
    mine = rows_ref[pl.ds(pl.multiple_of(table[0, b] * BLK, BLK), BLK), :width]
    queries = jnp.concatenate([mine[:, i * size : (i + 1) * size] for i in range(heads)], axis=0)
    spot = (b - first) * BLK
    row = lax.broadcasted_iota(jnp.int32, (heads, BLK, BLK), 1).reshape(heads * BLK, BLK) + spot
    col = lax.broadcasted_iota(jnp.int32, (heads * BLK, BLK), 1) + spot
    starts, keys, values, scores = [], [], [], []
    for i in range(OWN_BLK):
        start = pl.multiple_of(table[0, jnp.maximum(b - i, 0)] * BLK, BLK)
        key = rows_ref[pl.ds(start, BLK), width : width + size]
        col_i = col - i * BLK
        allowed = (col_i <= row) & (col_i < length) & (col_i >= 0)
        score = times_transpose(queries, key) * size ** (-0.5)
        starts.append(start)
        keys.append(key)
        values.append(rows_ref[pl.ds(start, BLK), width + size : width + 2 * size])
        scores.append(jnp.where(allowed, score, NEGATIVE))
    highest = scores[0]
    for score in scores[1:]:
        highest = jnp.maximum(highest, score)
    highest = jnp.max(highest, axis=-1, keepdims=True)
    powers = [jnp.exp(score - highest) for score in scores]
    total = powers[0]
    for power in powers[1:]:
        total = total + power
    total = jnp.sum(total, axis=-1, keepdims=True)
    weights = [power / total for power in powers]
    return mine, queries, starts, keys, values, weights


def forward_kernel(heads, size, table, rows_ref, out_ref):
    def step(b, carry):
        _, _, starts, _, values, weights = window(table, rows_ref, b, heads, size)
        mixed = dot(weights[0].astype(BF16), values[0])
        for weight, value in zip(weights[1:], values[1:]):
            mixed = mixed + dot(weight.astype(BF16), value)
        for i in range(heads):
            out_ref[pl.ds(starts[0], BLK), i * size : (i + 1) * size] = mixed[
                i * BLK : (i + 1) * BLK
            ].astype(BF16)
        return carry

    lax.fori_loop(0, table.shape[1], step, 0)


def backward_kernel(heads, size, table, rows_ref, grad_ref, out_ref, sums):
    sums[...] = jnp.zeros_like(sums)
    scale = size ** (-0.5)

    def step(b, carry):
        _, queries, starts, keys, values, weights = window(table, rows_ref, b, heads, size)
        grads = grad_ref[pl.ds(starts[0], BLK), :]
        grads = jnp.concatenate([grads[:, i * size : (i + 1) * size] for i in range(heads)], axis=0)
        pulls = [times_transpose(grads, value) for value in values]
        total = weights[0] * pulls[0]
        for weight, pull in zip(weights[1:], pulls[1:]):
            total = total + weight * pull
        total = jnp.sum(total, axis=-1, keepdims=True)
        grad_query = None
        for i in range(OWN_BLK):
            grad_score = (weights[i] * (pulls[i] - total)).astype(BF16)
            part = dot(grad_score, keys[i])
            grad_query = part if grad_query is None else grad_query + part
            spot = pl.ds(starts[i], BLK)
            sums[spot, :size] += outer_sum(grad_score, queries) * scale
            sums[spot, size:] += outer_sum(weights[i].astype(BF16), grads)
        for i in range(heads):
            out_ref[pl.ds(starts[0], BLK), i * size : (i + 1) * size] = (
                grad_query[i * BLK : (i + 1) * BLK] * scale
            ).astype(BF16)
        return carry

    lax.fori_loop(0, table.shape[1], step, 0)
    out_ref[:, heads * size :] = sums[...].astype(BF16)


def attend(table, rows, heads, size):
    return pl.pallas_call(
        functools.partial(forward_kernel, heads, size),
        out_shape=jax.ShapeDtypeStruct((rows.shape[0], heads * size), BF16),
        in_specs=[
            pl.BlockSpec(memory_space=pltpu.SMEM),
            pl.BlockSpec(memory_space=pltpu.VMEM),
        ],
        out_specs=pl.BlockSpec(memory_space=pltpu.VMEM),
        name="attend",
    )(table, rows)


def attend_back(table, rows, grads, heads, size):
    return pl.pallas_call(
        functools.partial(backward_kernel, heads, size),
        out_shape=jax.ShapeDtypeStruct(rows.shape, BF16),
        in_specs=[
            pl.BlockSpec(memory_space=pltpu.SMEM),
            pl.BlockSpec(memory_space=pltpu.VMEM),
            pl.BlockSpec(memory_space=pltpu.VMEM),
        ],
        out_specs=pl.BlockSpec(memory_space=pltpu.VMEM),
        scratch_shapes=[pltpu.VMEM((rows.shape[0], 2 * size), F32)],
        name="attend_back",
    )(table, rows, grads)


def unit_rows(values):
    return lax.rsqrt(jnp.mean(values * values, axis=-1, keepdims=True) + EPSILON)


def finish_kernel(sizes, order, raw_ref, cos_ref, sin_ref, gains_ref, out_ref):
    value_heads, group_heads, size = sizes
    per_group = group_heads * size
    query_width = value_heads * per_group
    key_width = value_heads * size

    def turned(start, gain):
        values = raw_ref[:, start : start + size]
        values = values * unit_rows(values) * gain
        return (
            values * cos_ref[...] + pltpu.roll(values, size // 2, 1) * sin_ref[...]
        ).astype(BF16)

    for head in range(value_heads):
        for i in range(group_heads):
            start = head * per_group + i * size
            out_ref[0, head, :, i * size : (i + 1) * size] = turned(start, gains_ref[0:1, :])
        start = query_width + head * size
        out_ref[0, head, :, per_group : per_group + size] = turned(start, gains_ref[1:2, :])
        start = query_width + key_width + head * size
        out_ref[0, head, :, per_group + size :] = raw_ref[:, start : start + size].astype(BF16)


def unfinish_kernel(
    sizes, order, raw_ref, grad_ref, cos_ref, sin_ref, gains_ref, out_ref, sums_ref
):
    value_heads, group_heads, size = sizes
    per_group = group_heads * size
    query_width = value_heads * per_group
    key_width = value_heads * size

    @pl.when(pl.program_id(0) == 0)
    def _():
        sums_ref[...] = jnp.zeros_like(sums_ref)

    def pull(grad, start, which):
        grad = grad.astype(F32)
        values = raw_ref[:, start : start + size]
        unit = unit_rows(values)
        values = values * unit
        grad = grad * cos_ref[...] + pltpu.roll(grad * sin_ref[...], size // 2, 1)
        sums_ref[which * 8 : which * 8 + 8, :] += jnp.sum(
            (grad * values).reshape(-1, 8, size), axis=0
        )
        grad = grad * gains_ref[which : which + 1, :]
        grad = unit * (grad - values * jnp.mean(grad * values, axis=-1, keepdims=True))
        out_ref[:, start : start + size] = grad.astype(BF16)

    for head in range(value_heads):
        for i in range(group_heads):
            pull(
                grad_ref[0, head, :, i * size : (i + 1) * size], head * per_group + i * size, 0
            )
        pull(grad_ref[0, head, :, per_group : per_group + size], query_width + head * size, 1)
        start = query_width + key_width + head * size
        out_ref[:, start : start + size] = grad_ref[0, head, :, per_group + size :]


def pack_kernel(heads, order, rows_ref, out_ref):
    width = out_ref.shape[3]
    for head in range(heads):
        out_ref[0, head] = rows_ref[:, head * width : (head + 1) * width]


def unpack_kernel(heads, order, pieces_ref, out_ref):
    width = pieces_ref.shape[3]
    for head in range(heads):
        out_ref[:, head * width : (head + 1) * width] = pieces_ref[0, head]


def row_spec(rows, cols):
    return pl.BlockSpec((rows, cols), lambda i, order: (i, 0))


def whole_spec(shape):
    return pl.BlockSpec(shape, lambda i, order: (0,) * len(shape))


def piece_spec(heads, rows, cols):
    return pl.BlockSpec((1, heads, rows, cols), lambda i, order: (order[i], 0, 0, 0))


def by_rows(kernel, name, order, args, in_specs, out_shape, out_specs, cost):
    return pl.pallas_call(
        kernel,
        grid_spec=pltpu.PrefetchScalarGridSpec(
            num_scalar_prefetch=1, grid=(NARROW,), in_specs=in_specs, out_specs=out_specs
        ),
        out_shape=out_shape,
        cost_estimate=pl.CostEstimate(flops=cost, bytes_accessed=cost, transcendentals=0),
        name=name,
    )(order, *args)


def finish(sizes, order, raw, cosines, sines, gains):
    value_heads, group_heads, size = sizes
    rows = raw.shape[0] // NARROW
    width = (group_heads + 2) * size
    return by_rows(
        functools.partial(finish_kernel, sizes),
        "finish",
        order,
        (raw, cosines, sines, gains),
        [
            row_spec(rows, raw.shape[1]),
            row_spec(rows, size),
            row_spec(rows, size),
            whole_spec(gains.shape),
        ],
        jax.ShapeDtypeStruct((NARROW, value_heads, rows, width), BF16),
        piece_spec(value_heads, rows, width),
        8 << 20,
    )


def unfinish(sizes, order, raw, pieces, cosines, sines, gains):
    value_heads, group_heads, size = sizes
    rows = raw.shape[0] // NARROW
    return by_rows(
        functools.partial(unfinish_kernel, sizes),
        "unfinish",
        order,
        (raw, pieces, cosines, sines, gains),
        [
            row_spec(rows, raw.shape[1]),
            piece_spec(value_heads, rows, pieces.shape[3]),
            row_spec(rows, size),
            row_spec(rows, size),
            whole_spec(gains.shape),
        ],
        (
            jax.ShapeDtypeStruct(raw.shape, BF16),
            jax.ShapeDtypeStruct((16, size), F32),
        ),
        (row_spec(rows, raw.shape[1]), whole_spec((16, size))),
        8 << 20,
    )


def pack(heads, order, values):
    rows = values.shape[0] // NARROW
    width = values.shape[1] // heads
    return by_rows(
        functools.partial(pack_kernel, heads),
        "pack",
        order,
        (values,),
        [row_spec(rows, values.shape[1])],
        jax.ShapeDtypeStruct((NARROW, heads, rows, width), BF16),
        piece_spec(heads, rows, width),
        2 << 20,
    )


def unpack(order, pieces):
    heads, rows, width = pieces.shape[1:]
    return by_rows(
        functools.partial(unpack_kernel, heads),
        "unpack",
        order,
        (pieces,),
        [piece_spec(heads, rows, width)],
        jax.ShapeDtypeStruct((NARROW * rows, heads * width), BF16),
        row_spec(rows, heads * width),
        2 << 20,
    )


def split_kernel(block, gate_ref, up_ref, out_ref):
    places = gate_ref.shape[1] // (block * NARROW)
    half = out_ref.shape[2] // 2
    for i, ref in enumerate((gate_ref, up_ref)):
        for n in range(NARROW):
            for place in range(places):
                chunk, spot = divmod(place, places // 2)
                start = chunk * half + i * (half // 2) + spot * block
                source = (place * NARROW + n) * block
                out_ref[n, :, start : start + block] = ref[:, source : source + block]


def merge_kernel(block, first_ref, second_ref, gate_ref, up_ref):
    places = gate_ref.shape[1] // (block * NARROW)
    half = first_ref.shape[2]
    for i, ref in enumerate((gate_ref, up_ref)):
        for n in range(NARROW):
            for place in range(places):
                chunk, spot = divmod(place, places // 2)
                source = (first_ref, second_ref)[chunk]
                start = i * (half // 2) + spot * block
                target = (place * NARROW + n) * block
                ref[:, target : target + block] = source[n, :, start : start + block].astype(F32)


def split_columns(block, gate, up):
    rows, cols = gate.shape
    if block % 64:
        def by_chunk(values):
            values = values.reshape(rows, 2, -1, NARROW, block).transpose(3, 0, 1, 2, 4)
            return values.reshape(NARROW, rows, 2, -1)

        both = jnp.concatenate([by_chunk(gate), by_chunk(up)], axis=3)
        return both.reshape(NARROW, rows, -1)
    return pl.pallas_call(
        functools.partial(split_kernel, block),
        out_shape=jax.ShapeDtypeStruct((NARROW, rows, 2 * cols // NARROW), BF16),
        name="split_columns",
    )(gate, up)


def merge_columns(block, first, second):
    rows, half = first.shape[1:]
    cols = half * NARROW
    if block % 64:
        both = jnp.stack([first, second], axis=2).reshape(NARROW, rows, 2, 2, -1, block)
        both = both.transpose(3, 1, 2, 4, 0, 5).reshape(2, rows, cols).astype(F32)
        return both[0], both[1]
    return pl.pallas_call(
        functools.partial(merge_kernel, block),
        out_shape=(jax.ShapeDtypeStruct((rows, cols), F32),) * 2,
        name="merge_columns",
    )(first, second)


def body(
    tokens,
    out_grad,
    attn_norm,
    w_query,
    key_weight,
    value_weight,
    query_norm,
    key_norm_gain,
    w_out,
    mlp_norm,
    w_gate,
    w_up,
    w_down,
    doc_blocks,
    doc_tail,
    doc_order,
    block_home,
):
    wide_count = lax.axis_size("wide")
    my_wide = lax.axis_index("wide")
    me = lax.axis_index("narrow")
    device_count = wide_count * NARROW
    ring = Ring(wide_count)
    rows = tokens.shape[0]
    block_count = rows // BLK
    head_size = query_norm.shape[0] * device_count
    query_width = w_query.shape[1] // NARROW
    key_width = key_weight.shape[1] // NARROW
    value_heads = key_width // head_size
    group_heads = query_width // key_width
    hidden = w_gate.shape[1] // NARROW
    shard = w_query.shape[0]
    parts = wide_count // (NARROW * value_heads)

    order = me ^ jnp.arange(NARROW, dtype=jnp.int32)
    sizes = (value_heads, group_heads, head_size)

    def narrow_exchange(pieces):
        pieces = jnp.take(pieces, order, axis=0)
        moved = [pieces[0]] + [swap(pieces[i], i) for i in range(1, NARROW)]
        return jnp.take(jnp.stack(moved), order, axis=0)

    def narrow_columns(weight):
        return weight.reshape(shard, NARROW, -1).transpose(1, 0, 2)

    def pad_lanes(values, size):
        return jnp.concatenate([values, jnp.zeros((size - values.shape[0],), BF16)])

    projection_width = query_width + 2 * key_width
    gains = [pad_lanes(gain, shard) for gain in (attn_norm, mlp_norm, query_norm, key_norm_gain)]
    gains = pad_lanes(jnp.concatenate(gains), projection_width)[None, :]
    extra = 32
    at_row = lax.broadcasted_iota(jnp.int32, (extra, projection_width), 0) == me
    gain_rows = jnp.broadcast_to(jnp.where(at_row, gains, 0)[None], (NARROW, extra, projection_width))
    first_pieces = jnp.concatenate(
        [narrow_columns(w_query), narrow_columns(key_weight), narrow_columns(value_weight)], axis=2
    )
    first_pieces = narrow_exchange(jnp.concatenate([first_pieces, gain_rows], axis=1))
    tokens_across = swap(tokens, 2)
    moves = [(g, (g % wide_count) * NARROW + g // wide_count) for g in range(device_count)]
    moves_back = [(b, a) for a, b in moves]
    out_part = lax.ppermute(w_out, DEVICES, moves)
    folds = w_out.shape[1] // projection_width
    out_part = out_part.reshape(shard, folds, -1).transpose(1, 0, 2).reshape(folds * shard, -1)
    gain_rows = jnp.sum(first_pieces[:, shard:].astype(F32), axis=0).astype(BF16)
    first_part = jnp.concatenate(
        [first_pieces[:, :shard].reshape(NARROW * shard, -1), out_part, gain_rows], axis=0
    )
    block = w_down.shape[0]
    first_ring = Gather(ring, first_part)
    down_ring = Gather(ring, w_down)
    begun = first_ring.advance(down_ring.advance())
    first_ring.advance(tokens_across)
    gate_part, up_part = tie((w_gate, w_up), begun)
    gate_up_pieces = split_columns(block, gate_part, up_part)
    gate_up_part = narrow_exchange(gate_up_pieces).reshape(NARROW * shard, -1)
    first_ring.advance()
    first_done = first_ring.advance()
    gathered = first_ring.whole.reshape(wide_count, -1, projection_width)
    projection = gathered[:, : NARROW * shard].reshape(-1, projection_width)
    out_rows = gathered[:, NARROW * shard : (NARROW + folds) * shard]
    out_rows = out_rows.reshape(wide_count, folds, shard, -1).transpose(0, 2, 1, 3)
    out_weight = out_rows.reshape(wide_count * shard, -1)
    gain_rows = gathered[:, (NARROW + folds) * shard :][:, :NARROW, : 4 * shard]
    gain_rows = gain_rows.reshape(device_count, 4, shard).astype(F32)
    attention_gain, mlp_gain = gain_rows[:, 0].reshape(-1), gain_rows[:, 1].reshape(-1)
    few = query_norm.shape[0]
    norm_gains = jnp.stack(
        [gain_rows[:, 2, :few].reshape(head_size), gain_rows[:, 3, :few].reshape(head_size)]
    )
    norm_gains = jnp.concatenate([norm_gains, jnp.zeros((6, head_size), F32)])
    rings = [Gather(ring, gate_up_part[:, :hidden]), Gather(ring, gate_up_part[:, hidden:])]

    inputs = tokens.astype(F32)
    all_inputs = narrow_gather(tokens, tokens_across)[0].astype(F32)
    normed = row_normalize(all_inputs, attention_gain).astype(BF16)
    raw = dot(normed, projection)
    owner_start, offsets = layout(
        doc_blocks, doc_order, tie(block_home, begun), my_wide, block_count
    )
    my_offsets = jnp.take(offsets, order, axis=0)
    position = (
        my_offsets.reshape(-1, 1) * BLK + jnp.arange(BLK, dtype=jnp.int32)[None, :]
    ).reshape(-1)
    half_size = head_size // 2
    frequency = THETA ** (-2.0 * jnp.arange(half_size, dtype=F32) / head_size)
    angles = position.astype(F32)[:, None] * frequency[None, :]
    cosines, sines = jnp.cos(angles), jnp.sin(angles)
    cosines = jnp.concatenate([cosines, cosines], axis=-1)
    sines = jnp.concatenate([-sines, sines], axis=-1)

    def exchange(pieces):
        pieces = jnp.broadcast_to(
            pieces[:, :, None], pieces.shape[:2] + (parts,) + pieces.shape[2:]
        ).reshape(wide_count, rows, -1)
        return lax.all_to_all(pieces, "wide", split_axis=0, concat_axis=0, tiled=True).reshape(
            wide_count * rows, -1
        )

    def exchange_back(values):
        pieces = lax.all_to_all(
            values.reshape(wide_count, rows, -1), "wide", split_axis=0, concat_axis=0, tiled=True
        )
        return pieces.reshape(NARROW, value_heads, parts, rows, -1)[:, :, 0]

    finished = finish(sizes, order, raw, cosines, sines, norm_gains)
    arrived = exchange(tie(finished, down_ring.advance(first_done)))
    table = stream_table(
        my_wide // (wide_count // NARROW), owner_start, doc_blocks, doc_tail, block_home, block_count
    )
    arrived = tie(arrived, rings[0].advance(first_done), down_ring.advance(finished))
    attended = tie(attend(table, arrived, group_heads, head_size), rings[0].advance(arrived))
    mixed = exchange_back(attended)
    third = rings[0].advance(attended)
    mixed = unpack(order, tie(mixed, down_ring.advance(attended)))

    reduced, unused_near, across = narrow_reduce(dot(mixed, out_weight))
    fourth = rings[0].advance(mixed)
    middle = inputs + tie(reduced, third)
    begun = rings[1].advance(across)
    normed_two, across = narrow_gather(row_normalize(middle, mlp_gain).astype(BF16))
    all_out_grad, unused_across = narrow_gather(tie(out_grad, mixed))
    normed_two = tie(normed_two, fourth, all_out_grad)
    second = rings[1].advance(across)
    down = down_ring.whole
    part = hidden // 2

    def half_forward(rows, weights):
        gate_sum, up_sum = dot(rows, weights[:, :part]), dot(rows, weights[:, part:])
        return gate_sum, up_sum, gated(gate_sum, up_sum).astype(BF16)

    def half_back(gate_sum, up_sum, grad_hidden):
        unused_gated, pull = jax.vjp(gated, gate_sum, up_sum)
        return jnp.concatenate([grad.astype(BF16) for grad in pull(grad_hidden)], axis=1)

    gate_sum, up_sum, hidden_first = half_forward(normed_two, rings[0].whole)
    wait_first = tie(all_out_grad, hidden_first, second)
    grad_first = half_back(gate_sum, up_sum, times_transpose(wait_first, down[:part]))
    third = rings[1].advance(hidden_first)
    first_half_terms = outer_sum(normed_two, tie(grad_first, third)).astype(BF16)
    first_half = Reduce(ring, first_half_terms)
    wait_second = tie(normed_two, first_half_terms, rings[1].advance(grad_first))
    gate_sum, up_sum, hidden_second = half_forward(wait_second, rings[1].whole)
    wait_second = tie(all_out_grad, hidden_second, first_half.advance())
    grad_second = half_back(gate_sum, up_sum, times_transpose(wait_second, down[part:]))
    early = first_half.advance(hidden_second)
    grad_first = tie(grad_first, grad_second)
    grad_terms = (
        times_transpose(grad_first, rings[0].whole) + times_transpose(grad_second, rings[1].whole)
    ).astype(BF16)
    grad_terms = tie(grad_terms, early)
    grad_normed_two, near, across = narrow_reduce(grad_terms)
    third = first_half.advance(grad_terms)
    later_grad, later_normed, hidden_rows = tie(
        (grad_second, normed_two, (hidden_first, hidden_second)), near
    )
    hidden_rows = jnp.concatenate(hidden_rows, axis=1)
    second_half_terms = outer_sum(later_normed, later_grad).astype(BF16)
    second_half = Reduce(ring, second_half_terms)
    down_terms = outer_sum(hidden_rows, all_out_grad).astype(BF16)
    grad_normed_two = tie(grad_normed_two, third, second_half_terms, down_terms)
    unused_norm, second_pull = jax.vjp(lambda value: row_normalize(value, mlp_gain), middle)
    grad_middle = out_grad.astype(F32) + second_pull(grad_normed_two)[0]

    early = [first_half.advance(across), second_half.advance(across)]
    grad_branch, across = narrow_gather(grad_middle.astype(BF16))
    grad_mixed = times_transpose(grad_branch, out_weight).astype(BF16)
    grad_pack = tie(pack(value_heads, order, grad_mixed), early)
    second = second_half.advance(across)
    later_branch, later_hidden = tie((grad_branch, hidden_rows), grad_pack)
    arrived_grad = exchange(grad_pack)

    def narrow_rows(share):
        return narrow_exchange(share.astype(BF16).reshape(NARROW, shard, -1))

    last_sums = Reduce(ring, down_terms, outer_sum(mixed, later_branch).astype(BF16))
    arrived_grad = tie(arrived_grad, second, last_sums.advance())
    third = second_half.advance(arrived_grad)
    grad_pieces = attend_back(table, arrived, arrived_grad, group_heads, head_size)
    grad_pieces = tie(grad_pieces, third)
    first_rows = narrow_rows(tie(first_half.result(), arrived_grad))
    output = (middle + narrow_reduce(dot(later_hidden, down))[0]).astype(BF16)
    early = [second_half.advance(grad_pieces), last_sums.advance(grad_pieces)]
    grad_pieces = tie(exchange_back(grad_pieces), early, first_rows, output)
    projection_grad, norm_sums = unfinish(
        sizes, order, raw, grad_pieces, cosines, sines, norm_gains
    )
    third = last_sums.advance(grad_pieces)
    first_terms = outer_sum(normed, projection_grad).astype(BF16)
    norm_terms = jnp.pad(
        norm_sums.astype(BF16), ((0, extra - 16), (0, projection_width - head_size))
    )
    first_sums = Reduce(ring, first_terms, shared=norm_terms)
    grad_normed, near, across = narrow_reduce(
        times_transpose(tie(projection_grad, first_terms), projection)
    )
    first_sums.advance()
    second_rows = narrow_rows(tie(second_half.result(), first_terms))
    last_sums.advance(first_terms)
    first_sums.advance(near)
    first_sums.advance(across, third)
    w_gate_grad, w_up_grad = merge_columns(block, first_rows, second_rows)
    first_sums.advance(second_rows)
    unused_first, first_pull = jax.vjp(lambda value: row_normalize(value, attention_gain), inputs)
    tokens_grad = (grad_middle + first_pull(grad_normed)[0]).astype(BF16)

    def all_columns(pieces):
        return pieces.astype(F32).transpose(1, 0, 2).reshape(shard, -1)

    share = first_sums.result().astype(BF16)
    norm_rows = share[NARROW * shard :][:16]
    norm_rows = jnp.broadcast_to(norm_rows[None], (NARROW,) + norm_rows.shape)
    projection_rows = narrow_exchange(
        jnp.concatenate([share[: NARROW * shard].reshape(NARROW, shard, -1), norm_rows], axis=1)
    )
    norm_grads = jnp.sum(projection_rows[:, shard:, :head_size].astype(F32), axis=0)
    norm_grads = jnp.sum(norm_grads.reshape(2, 8, head_size), axis=1)
    projection_rows = projection_rows[:, :shard]
    w_query_grad = all_columns(projection_rows[:, :, :query_width])
    w_key_grad = all_columns(projection_rows[:, :, query_width : query_width + key_width])
    w_value_grad = all_columns(projection_rows[:, :, query_width + key_width :])
    last_share = last_sums.result()
    w_down_grad = last_share[:block]
    w_out_grad = lax.ppermute(last_share[block:].astype(BF16), DEVICES, moves_back).astype(F32)

    def row_sums(pairs):
        total = 0.0
        for weight, grad in pairs:
            total = total + jnp.sum(weight.astype(F32) * grad, axis=1)
        return total

    attn_norm_grad = row_sums(
        [(w_query, w_query_grad), (key_weight, w_key_grad), (value_weight, w_value_grad)]
    ) / attn_norm.astype(F32)
    mlp_norm_grad = row_sums([(w_gate, w_gate_grad), (w_up, w_up_grad)]) / mlp_norm.astype(F32)
    mine = lax.dynamic_slice(norm_grads, (0, (my_wide * NARROW + me) * few), (2, few))
    return (
        output,
        tokens_grad,
        attn_norm_grad,
        w_query_grad,
        w_key_grad,
        w_value_grad,
        mine[0],
        mine[1],
        w_out_grad,
        mlp_norm_grad,
        w_gate_grad,
        w_up_grad,
        w_down_grad,
    )


def solution(mesh):
    rows = P(DEVICES, None)
    vector = P(DEVICES)
    in_specs = (
        (rows, rows, vector, rows, rows, rows, vector, vector, rows, vector, rows, rows, rows)
        + (P(),) * 4
    )
    out_specs = (
        (rows, rows, vector, rows, rows, rows, vector, vector, rows, vector, rows, rows, rows)
    )
    return jax.shard_map(body, mesh=mesh, in_specs=in_specs, out_specs=out_specs, check_vma=False)
```

```python
import functools

import jax
import jax.numpy as jnp
import numpy as np
from jax import lax
from jax.experimental import pallas as pl
from jax.experimental.pallas import tpu as pltpu
from jax.sharding import PartitionSpec as P

BLK = 128
OWN_BLK = 4
EPSILON = 1e-06
THETA = 1000000.0
LANES = 128
NARROW = 4
CONTRACT_ROWS = (((0,), (0,)), ((), ()))
CONTRACT_COLS = (((1,), (1,)), ((), ()))
NEGATIVE = -1e30
F32 = jnp.float32
BF16 = jnp.bfloat16
DEVICES = ("wide", "narrow")


def row_normalize(values, gain_row):
    return (
        values * lax.rsqrt(jnp.mean(values * values, axis=-1, keepdims=True) + EPSILON) * gain_row
    )


def gated(gate_sum, up_sum):
    return jax.nn.silu(gate_sum) * up_sum


def dot(left, right):
    return jnp.dot(left, right, preferred_element_type=F32)


def outer_sum(left_rows, right_rows):
    return lax.dot_general(left_rows, right_rows, CONTRACT_ROWS, preferred_element_type=F32)


def times_transpose(left_rows, matrix):
    return lax.dot_general(left_rows, matrix, CONTRACT_COLS, preferred_element_type=F32)


def ring_order(count):
    rows = count // 2
    return [2 * i for i in range(rows)] + [2 * i + 1 for i in reversed(range(rows))]


class Ring:
    def __init__(self, count):
        self.count = count
        order = ring_order(count)
        place = np.zeros(count, np.int32)
        for i, device in enumerate(order):
            place[device] = i
        self.onward = [(order[i], order[(i + 1) % count]) for i in range(count)]
        self.back = [(b, a) for a, b in self.onward]
        self.order = jnp.asarray(np.array(order + order + order, np.int32))
        self.place = jnp.asarray(place)[lax.axis_index("wide")]

    def device(self, shift):
        return self.order[self.place + self.count + shift]

    def send(self, value, forward):
        return lax.ppermute(value, "wide", self.onward if forward else self.back)


def no_op(out_ref):
    pass


def blank(shape, dtype):
    return pl.pallas_call(
        no_op,
        out_shape=jax.ShapeDtypeStruct(shape, dtype),
        out_specs=pl.BlockSpec(memory_space=pl.ANY),
    )()


def tie(value, *after):
    after = [leaf for leaf in jax.tree.leaves(after)]
    return lax.optimization_barrier((value, after))[0] if after else value


class Gather:
    def __init__(self, ring, part):
        self.ring, self.rows, self.step, self.flight = ring, part.shape[0], 0, []
        self.ahead, self.behind = part, part
        if ring.count > 8:
            self.whole = lax.all_gather(part, "wide", axis=0, tiled=True)
        else:
            self.whole = self.put(
                blank((ring.count * self.rows, part.shape[1]), part.dtype), part, 0, 0
            )

    def put(self, whole, value, shift, extra):
        return lax.dynamic_update_slice(
            whole, value, (self.ring.device(shift) * self.rows + extra, 0)
        )

    def advance(self, *after):
        ring, half = self.ring, self.rows // 2
        if ring.count > 8:
            return []
        self.step += 1
        last = self.step == ring.count // 2
        ahead, behind = tie((self.ahead, self.behind), after)
        if last:
            ahead, behind = ahead[:half], behind[half:]
        self.ahead, self.behind = ring.send(ahead, True), ring.send(behind, False)
        self.whole = self.put(self.whole, self.ahead, -self.step, 0)
        self.whole = self.put(self.whole, self.behind, self.step, half if last else 0)
        return [self.ahead, self.behind]


class Reduce:
    def __init__(self, ring, *terms, shared=None):
        self.ring, self.terms, self.shared, self.step = ring, terms, shared, 0
        if ring.count > 8:
            parts = [term.reshape(ring.count, -1, term.shape[1]) for term in terms]
            if shared is not None:
                parts.append(jnp.broadcast_to(shared[None], (ring.count,) + shared.shape))
            whole = jnp.concatenate(parts, axis=1).reshape(-1, terms[0].shape[1])
            self.total = lax.psum_scatter(whole, "wide", scatter_dimension=0, tiled=True)

    def term(self, shift):
        parts = []
        for term in self.terms:
            rows = term.shape[0] // self.ring.count
            start = self.ring.device(shift) * rows
            parts.append(lax.dynamic_slice(term, (start, 0), (rows, term.shape[1])))
        if self.shared is not None:
            parts.append(self.shared)
        return parts[0] if len(parts) == 1 else jnp.concatenate(parts, axis=0)

    def advance(self, *after):
        ring = self.ring
        if ring.count > 8:
            return []
        shift = ring.count // 2 - self.step
        if self.step:
            ahead, behind = tie((self.ahead, self.behind), after)
            mine, other = self.term(shift), self.term(-shift)
            half = mine.shape[0] // 2
            if self.step == 1:
                ahead = jnp.concatenate([join(mine[:half], ahead), mine[half:]], axis=0)
                behind = jnp.concatenate([other[:half], join(other[half:], behind)], axis=0)
            else:
                ahead, behind = join(mine, ahead), join(other, behind)
        else:
            far = tie(self.term(shift), after)
            half = far.shape[0] // 2
            ahead, behind = far[:half], far[half:]
        self.step += 1
        self.ahead, self.behind = ring.send(ahead, True), ring.send(behind, False)
        return [self.ahead, self.behind]

    def result(self):
        if self.ring.count > 8:
            return self.total.astype(F32)
        return self.term(0).astype(F32) + self.ahead.astype(F32) + self.behind.astype(F32)


def join(left, right):
    return (left.astype(F32) + right.astype(F32)).astype(BF16)


def swap(value, bit):
    return lax.ppermute(value, "narrow", [(i, i ^ bit) for i in range(NARROW)])


def narrow_gather(value, across=None):
    across = swap(value, 2) if across is None else across
    return jnp.concatenate([value, swap(value, 1), across, swap(across, 1)], axis=0), across


def narrow_reduce(terms):
    rows = terms.shape[0] // NARROW
    low = terms.astype(BF16)
    parts = [low[i * rows : (i + 1) * rows] for i in range(NARROW)]
    near, far = swap(parts[1], 1), swap(parts[3], 1)
    across = swap(join(parts[2], far), 2)
    return parts[0].astype(F32) + near.astype(F32) + across.astype(F32), (near, far), across


def layout(doc_blocks, doc_order, block_home, my_wide, block_count):
    owners = doc_blocks.shape[1]
    owner_ids = jnp.arange(owners, dtype=jnp.int32)
    hits = (doc_order[:, :, None] == owner_ids[None, None, :]).astype(jnp.int32)
    in_stream = jnp.sum(hits * doc_blocks[:, None, :], axis=2)
    before = (owner_ids[:, None] < owner_ids[None, :]).astype(jnp.int32)
    stream_start = jnp.sum(in_stream[:, :, None] * before[None], axis=1)
    owner_start = jnp.sum(hits * stream_start[:, :, None], axis=1)
    column = jnp.sum(jnp.where(block_home == my_wide, owner_ids[None, :], 0), axis=1)
    stream_ids = jnp.arange(block_count, dtype=jnp.int32)[None, :] * owners + column[:, None]
    member = (owner_start[:, None, :] <= stream_ids[:, :, None]) & (
        stream_ids[:, :, None] < (owner_start + doc_blocks)[:, None, :]
    )
    offsets = stream_ids - jnp.sum(jnp.where(member, owner_start[:, None, :], 0), axis=2)
    return owner_start, offsets


def stream_table(group, owner_start, doc_blocks, doc_tail, block_home, block_count):
    def pick(table):
        return lax.dynamic_index_in_dim(table, group, 0, keepdims=False)

    starts, blocks, tails, homes = pick(owner_start), pick(doc_blocks), pick(doc_tail), pick(block_home)
    owners = starts.shape[0]
    ids = jnp.arange(owners * block_count, dtype=jnp.int32)
    member = (starts[None, :] <= ids[:, None]) & (ids[:, None] < (starts + blocks)[None, :])

    def chosen(values):
        return jnp.sum(jnp.where(member, values[None, :], 0), axis=1)

    home = jnp.sum(
        jnp.where(
            (ids % owners)[:, None] == jnp.arange(owners, dtype=jnp.int32)[None, :],
            homes[None, :],
            0,
        ),
        axis=1,
    )
    place = home * block_count + ids // owners
    return jnp.stack([place, chosen(starts), chosen((blocks - 1) * BLK + tails)])


def window(table, rows_ref, b, heads, size):
    first, length = table[1, b], table[2, b]
    width = heads * size
    mine = rows_ref[pl.ds(pl.multiple_of(table[0, b] * BLK, BLK), BLK), :width]
    queries = jnp.concatenate([mine[:, i * size : (i + 1) * size] for i in range(heads)], axis=0)
    spot = (b - first) * BLK
    row = lax.broadcasted_iota(jnp.int32, (heads, BLK, BLK), 1).reshape(heads * BLK, BLK) + spot
    col = lax.broadcasted_iota(jnp.int32, (heads * BLK, BLK), 1) + spot
    starts, keys, values, scores = [], [], [], []
    for i in range(OWN_BLK):
        start = pl.multiple_of(table[0, jnp.maximum(b - i, 0)] * BLK, BLK)
        key = rows_ref[pl.ds(start, BLK), width : width + size]
        col_i = col - i * BLK
        allowed = (col_i <= row) & (col_i < length) & (col_i >= 0)
        score = times_transpose(queries, key) * size ** (-0.5)
        starts.append(start)
        keys.append(key)
        values.append(rows_ref[pl.ds(start, BLK), width + size : width + 2 * size])
        scores.append(jnp.where(allowed, score, NEGATIVE))
    highest = scores[0]
    for score in scores[1:]:
        highest = jnp.maximum(highest, score)
    highest = jnp.max(highest, axis=-1, keepdims=True)
    powers = [jnp.exp(score - highest) for score in scores]
    total = powers[0]
    for power in powers[1:]:
        total = total + power
    total = jnp.sum(total, axis=-1, keepdims=True)
    weights = [power / total for power in powers]
    return mine, queries, starts, keys, values, weights


def forward_kernel(heads, size, table, rows_ref, out_ref):
    def step(b, carry):
        _, _, starts, _, values, weights = window(table, rows_ref, b, heads, size)
        mixed = dot(weights[0].astype(BF16), values[0])
        for weight, value in zip(weights[1:], values[1:]):
            mixed = mixed + dot(weight.astype(BF16), value)
        for i in range(heads):
            out_ref[pl.ds(starts[0], BLK), i * size : (i + 1) * size] = mixed[
                i * BLK : (i + 1) * BLK
            ].astype(BF16)
        return carry

    lax.fori_loop(0, table.shape[1], step, 0)


def backward_kernel(heads, size, table, rows_ref, grad_ref, out_ref, sums):
    sums[...] = jnp.zeros_like(sums)
    scale = size ** (-0.5)

    def step(b, carry):
        _, queries, starts, keys, values, weights = window(table, rows_ref, b, heads, size)
        grads = grad_ref[pl.ds(starts[0], BLK), :]
        grads = jnp.concatenate([grads[:, i * size : (i + 1) * size] for i in range(heads)], axis=0)
        pulls = [times_transpose(grads, value) for value in values]
        total = weights[0] * pulls[0]
        for weight, pull in zip(weights[1:], pulls[1:]):
            total = total + weight * pull
        total = jnp.sum(total, axis=-1, keepdims=True)
        grad_query = None
        for i in range(OWN_BLK):
            grad_score = (weights[i] * (pulls[i] - total)).astype(BF16)
            part = dot(grad_score, keys[i])
            grad_query = part if grad_query is None else grad_query + part
            spot = pl.ds(starts[i], BLK)
            sums[spot, :size] += outer_sum(grad_score, queries) * scale
            sums[spot, size:] += outer_sum(weights[i].astype(BF16), grads)
        for i in range(heads):
            out_ref[pl.ds(starts[0], BLK), i * size : (i + 1) * size] = (
                grad_query[i * BLK : (i + 1) * BLK] * scale
            ).astype(BF16)
        return carry

    lax.fori_loop(0, table.shape[1], step, 0)
    out_ref[:, heads * size :] = sums[...].astype(BF16)


def attend(table, rows, heads, size):
    return pl.pallas_call(
        functools.partial(forward_kernel, heads, size),
        out_shape=jax.ShapeDtypeStruct((rows.shape[0], heads * size), BF16),
        in_specs=[
            pl.BlockSpec(memory_space=pltpu.SMEM),
            pl.BlockSpec(memory_space=pltpu.VMEM),
        ],
        out_specs=pl.BlockSpec(memory_space=pltpu.VMEM),
        name="attend",
    )(table, rows)


def attend_back(table, rows, grads, heads, size):
    return pl.pallas_call(
        functools.partial(backward_kernel, heads, size),
        out_shape=jax.ShapeDtypeStruct(rows.shape, BF16),
        in_specs=[
            pl.BlockSpec(memory_space=pltpu.SMEM),
            pl.BlockSpec(memory_space=pltpu.VMEM),
            pl.BlockSpec(memory_space=pltpu.VMEM),
        ],
        out_specs=pl.BlockSpec(memory_space=pltpu.VMEM),
        scratch_shapes=[pltpu.VMEM((rows.shape[0], 2 * size), F32)],
        name="attend_back",
    )(table, rows, grads)


def unit_rows(values):
    return lax.rsqrt(jnp.mean(values * values, axis=-1, keepdims=True) + EPSILON)


def finish_kernel(sizes, order, raw_ref, cos_ref, sin_ref, gains_ref, out_ref):
    value_heads, group_heads, size = sizes
    per_group = group_heads * size
    query_width = value_heads * per_group
    key_width = value_heads * size

    def turned(start, gain):
        values = raw_ref[:, start : start + size]
        values = values * unit_rows(values) * gain
        return (
            values * cos_ref[...] + pltpu.roll(values, size // 2, 1) * sin_ref[...]
        ).astype(BF16)

    for head in range(value_heads):
        for i in range(group_heads):
            start = head * per_group + i * size
            out_ref[0, head, :, i * size : (i + 1) * size] = turned(start, gains_ref[0:1, :])
        start = query_width + head * size
        out_ref[0, head, :, per_group : per_group + size] = turned(start, gains_ref[1:2, :])
        start = query_width + key_width + head * size
        out_ref[0, head, :, per_group + size :] = raw_ref[:, start : start + size].astype(BF16)


def unfinish_kernel(
    sizes, order, raw_ref, grad_ref, cos_ref, sin_ref, gains_ref, out_ref, sums_ref
):
    value_heads, group_heads, size = sizes
    per_group = group_heads * size
    query_width = value_heads * per_group
    key_width = value_heads * size

    @pl.when(pl.program_id(0) == 0)
    def _():
        sums_ref[...] = jnp.zeros_like(sums_ref)

    def pull(grad, start, which):
        grad = grad.astype(F32)
        values = raw_ref[:, start : start + size]
        unit = unit_rows(values)
        values = values * unit
        grad = grad * cos_ref[...] + pltpu.roll(grad * sin_ref[...], size // 2, 1)
        sums_ref[which * 8 : which * 8 + 8, :] += jnp.sum(
            (grad * values).reshape(-1, 8, size), axis=0
        )
        grad = grad * gains_ref[which : which + 1, :]
        grad = unit * (grad - values * jnp.mean(grad * values, axis=-1, keepdims=True))
        out_ref[:, start : start + size] = grad.astype(BF16)

    for head in range(value_heads):
        for i in range(group_heads):
            pull(
                grad_ref[0, head, :, i * size : (i + 1) * size], head * per_group + i * size, 0
            )
        pull(grad_ref[0, head, :, per_group : per_group + size], query_width + head * size, 1)
        start = query_width + key_width + head * size
        out_ref[:, start : start + size] = grad_ref[0, head, :, per_group + size :]


def pack_kernel(heads, order, rows_ref, out_ref):
    width = out_ref.shape[3]
    for head in range(heads):
        out_ref[0, head] = rows_ref[:, head * width : (head + 1) * width]


def unpack_kernel(heads, order, pieces_ref, out_ref):
    width = pieces_ref.shape[3]
    for head in range(heads):
        out_ref[:, head * width : (head + 1) * width] = pieces_ref[0, head]


def row_spec(rows, cols):
    return pl.BlockSpec((rows, cols), lambda i, order: (i, 0))


def whole_spec(shape):
    return pl.BlockSpec(shape, lambda i, order: (0,) * len(shape))


def piece_spec(heads, rows, cols):
    return pl.BlockSpec((1, heads, rows, cols), lambda i, order: (order[i], 0, 0, 0))


def by_rows(kernel, name, order, args, in_specs, out_shape, out_specs, cost):
    return pl.pallas_call(
        kernel,
        grid_spec=pltpu.PrefetchScalarGridSpec(
            num_scalar_prefetch=1, grid=(NARROW,), in_specs=in_specs, out_specs=out_specs
        ),
        out_shape=out_shape,
        cost_estimate=pl.CostEstimate(flops=cost, bytes_accessed=cost, transcendentals=0),
        name=name,
    )(order, *args)


def finish(sizes, order, raw, cosines, sines, gains):
    value_heads, group_heads, size = sizes
    rows = raw.shape[0] // NARROW
    width = (group_heads + 2) * size
    return by_rows(
        functools.partial(finish_kernel, sizes),
        "finish",
        order,
        (raw, cosines, sines, gains),
        [
            row_spec(rows, raw.shape[1]),
            row_spec(rows, size),
            row_spec(rows, size),
            whole_spec(gains.shape),
        ],
        jax.ShapeDtypeStruct((NARROW, value_heads, rows, width), BF16),
        piece_spec(value_heads, rows, width),
        8 << 20,
    )


def unfinish(sizes, order, raw, pieces, cosines, sines, gains):
    value_heads, group_heads, size = sizes
    rows = raw.shape[0] // NARROW
    return by_rows(
        functools.partial(unfinish_kernel, sizes),
        "unfinish",
        order,
        (raw, pieces, cosines, sines, gains),
        [
            row_spec(rows, raw.shape[1]),
            piece_spec(value_heads, rows, pieces.shape[3]),
            row_spec(rows, size),
            row_spec(rows, size),
            whole_spec(gains.shape),
        ],
        (
            jax.ShapeDtypeStruct(raw.shape, BF16),
            jax.ShapeDtypeStruct((16, size), F32),
        ),
        (row_spec(rows, raw.shape[1]), whole_spec((16, size))),
        8 << 20,
    )


def pack(heads, order, values):
    rows = values.shape[0] // NARROW
    width = values.shape[1] // heads
    return by_rows(
        functools.partial(pack_kernel, heads),
        "pack",
        order,
        (values,),
        [row_spec(rows, values.shape[1])],
        jax.ShapeDtypeStruct((NARROW, heads, rows, width), BF16),
        piece_spec(heads, rows, width),
        2 << 20,
    )


def unpack(order, pieces):
    heads, rows, width = pieces.shape[1:]
    return by_rows(
        functools.partial(unpack_kernel, heads),
        "unpack",
        order,
        (pieces,),
        [piece_spec(heads, rows, width)],
        jax.ShapeDtypeStruct((NARROW * rows, heads * width), BF16),
        row_spec(rows, heads * width),
        2 << 20,
    )


def split_kernel(block, gate_ref, up_ref, out_ref):
    places = gate_ref.shape[1] // (block * NARROW)
    half = out_ref.shape[2] // 2
    for i, ref in enumerate((gate_ref, up_ref)):
        for n in range(NARROW):
            for place in range(places):
                chunk, spot = divmod(place, places // 2)
                start = chunk * half + i * (half // 2) + spot * block
                source = (place * NARROW + n) * block
                out_ref[n, :, start : start + block] = ref[:, source : source + block]


def merge_kernel(block, first_ref, second_ref, gate_ref, up_ref):
    places = gate_ref.shape[1] // (block * NARROW)
    half = first_ref.shape[2]
    for i, ref in enumerate((gate_ref, up_ref)):
        for n in range(NARROW):
            for place in range(places):
                chunk, spot = divmod(place, places // 2)
                source = (first_ref, second_ref)[chunk]
                start = i * (half // 2) + spot * block
                target = (place * NARROW + n) * block
                ref[:, target : target + block] = source[n, :, start : start + block].astype(F32)


def split_columns(block, gate, up):
    rows, cols = gate.shape
    if block % 64:
        def by_chunk(values):
            values = values.reshape(rows, 2, -1, NARROW, block).transpose(3, 0, 1, 2, 4)
            return values.reshape(NARROW, rows, 2, -1)

        both = jnp.concatenate([by_chunk(gate), by_chunk(up)], axis=3)
        return both.reshape(NARROW, rows, -1)
    return pl.pallas_call(
        functools.partial(split_kernel, block),
        out_shape=jax.ShapeDtypeStruct((NARROW, rows, 2 * cols // NARROW), BF16),
        name="split_columns",
    )(gate, up)


def merge_columns(block, first, second):
    rows, half = first.shape[1:]
    cols = half * NARROW
    if block % 64:
        both = jnp.stack([first, second], axis=2).reshape(NARROW, rows, 2, 2, -1, block)
        both = both.transpose(3, 1, 2, 4, 0, 5).reshape(2, rows, cols).astype(F32)
        return both[0], both[1]
    return pl.pallas_call(
        functools.partial(merge_kernel, block),
        out_shape=(jax.ShapeDtypeStruct((rows, cols), F32),) * 2,
        name="merge_columns",
    )(first, second)


def body(
    tokens,
    out_grad,
    attn_norm,
    w_query,
    key_weight,
    value_weight,
    query_norm,
    key_norm_gain,
    w_out,
    mlp_norm,
    w_gate,
    w_up,
    w_down,
    doc_blocks,
    doc_tail,
    doc_order,
    block_home,
):
    wide_count = lax.axis_size("wide")
    my_wide = lax.axis_index("wide")
    me = lax.axis_index("narrow")
    device_count = wide_count * NARROW
    ring = Ring(wide_count)
    rows = tokens.shape[0]
    block_count = rows // BLK
    head_size = query_norm.shape[0] * device_count
    query_width = w_query.shape[1] // NARROW
    key_width = key_weight.shape[1] // NARROW
    value_heads = key_width // head_size
    group_heads = query_width // key_width
    hidden = w_gate.shape[1] // NARROW
    shard = w_query.shape[0]
    parts = wide_count // (NARROW * value_heads)

    order = me ^ jnp.arange(NARROW, dtype=jnp.int32)
    sizes = (value_heads, group_heads, head_size)

    def narrow_exchange(pieces):
        pieces = jnp.take(pieces, order, axis=0)
        moved = [pieces[0]] + [swap(pieces[i], i) for i in range(1, NARROW)]
        return jnp.take(jnp.stack(moved), order, axis=0)

    def narrow_columns(weight):
        return weight.reshape(shard, NARROW, -1).transpose(1, 0, 2)

    def pad_lanes(values, size):
        return jnp.concatenate([values, jnp.zeros((size - values.shape[0],), BF16)])

    projection_width = query_width + 2 * key_width
    gains = [pad_lanes(gain, shard) for gain in (attn_norm, mlp_norm, query_norm, key_norm_gain)]
    gains = pad_lanes(jnp.concatenate(gains), projection_width)[None, :]
    extra = 32
    at_row = lax.broadcasted_iota(jnp.int32, (extra, projection_width), 0) == me
    gain_rows = jnp.broadcast_to(jnp.where(at_row, gains, 0)[None], (NARROW, extra, projection_width))
    first_pieces = jnp.concatenate(
        [narrow_columns(w_query), narrow_columns(key_weight), narrow_columns(value_weight)], axis=2
    )
    first_pieces = narrow_exchange(jnp.concatenate([first_pieces, gain_rows], axis=1))
    tokens_across = swap(tokens, 2)
    moves = [(g, (g % wide_count) * NARROW + g // wide_count) for g in range(device_count)]
    moves_back = [(b, a) for a, b in moves]
    out_part = lax.ppermute(w_out, DEVICES, moves)
    folds = w_out.shape[1] // projection_width
    out_part = out_part.reshape(shard, folds, -1).transpose(1, 0, 2).reshape(folds * shard, -1)
    gain_rows = jnp.sum(first_pieces[:, shard:].astype(F32), axis=0).astype(BF16)
    first_part = jnp.concatenate(
        [first_pieces[:, :shard].reshape(NARROW * shard, -1), out_part, gain_rows], axis=0
    )
    block = w_down.shape[0]
    first_ring = Gather(ring, first_part)
    down_ring = Gather(ring, w_down)
    begun = first_ring.advance(down_ring.advance())
    first_ring.advance(tokens_across)
    gate_part, up_part = tie((w_gate, w_up), begun)
    gate_up_pieces = split_columns(block, gate_part, up_part)
    gate_up_part = narrow_exchange(gate_up_pieces).reshape(NARROW * shard, -1)
    first_ring.advance()
    first_done = first_ring.advance()
    gathered = first_ring.whole.reshape(wide_count, -1, projection_width)
    projection = gathered[:, : NARROW * shard].reshape(-1, projection_width)
    out_rows = gathered[:, NARROW * shard : (NARROW + folds) * shard]
    out_rows = out_rows.reshape(wide_count, folds, shard, -1).transpose(0, 2, 1, 3)
    out_weight = out_rows.reshape(wide_count * shard, -1)
    gain_rows = gathered[:, (NARROW + folds) * shard :][:, :NARROW, : 4 * shard]
    gain_rows = gain_rows.reshape(device_count, 4, shard).astype(F32)
    attention_gain, mlp_gain = gain_rows[:, 0].reshape(-1), gain_rows[:, 1].reshape(-1)
    few = query_norm.shape[0]
    norm_gains = jnp.stack(
        [gain_rows[:, 2, :few].reshape(head_size), gain_rows[:, 3, :few].reshape(head_size)]
    )
    norm_gains = jnp.concatenate([norm_gains, jnp.zeros((6, head_size), F32)])
    rings = [Gather(ring, gate_up_part[:, :hidden]), Gather(ring, gate_up_part[:, hidden:])]

    inputs = tokens.astype(F32)
    all_inputs = narrow_gather(tokens, tokens_across)[0].astype(F32)
    normed = row_normalize(all_inputs, attention_gain).astype(BF16)
    raw = dot(normed, projection)
    owner_start, offsets = layout(
        doc_blocks, doc_order, tie(block_home, begun), my_wide, block_count
    )
    my_offsets = jnp.take(offsets, order, axis=0)
    position = (
        my_offsets.reshape(-1, 1) * BLK + jnp.arange(BLK, dtype=jnp.int32)[None, :]
    ).reshape(-1)
    half_size = head_size // 2
    frequency = THETA ** (-2.0 * jnp.arange(half_size, dtype=F32) / head_size)
    angles = position.astype(F32)[:, None] * frequency[None, :]
    cosines, sines = jnp.cos(angles), jnp.sin(angles)
    cosines = jnp.concatenate([cosines, cosines], axis=-1)
    sines = jnp.concatenate([-sines, sines], axis=-1)

    def exchange(pieces):
        pieces = jnp.broadcast_to(
            pieces[:, :, None], pieces.shape[:2] + (parts,) + pieces.shape[2:]
        ).reshape(wide_count, rows, -1)
        return lax.all_to_all(pieces, "wide", split_axis=0, concat_axis=0, tiled=True).reshape(
            wide_count * rows, -1
        )

    def exchange_back(values):
        pieces = lax.all_to_all(
            values.reshape(wide_count, rows, -1), "wide", split_axis=0, concat_axis=0, tiled=True
        )
        return pieces.reshape(NARROW, value_heads, parts, rows, -1)[:, :, 0]

    finished = finish(sizes, order, raw, cosines, sines, norm_gains)
    arrived = exchange(tie(finished, down_ring.advance(first_done)))
    table = stream_table(
        my_wide // (wide_count // NARROW), owner_start, doc_blocks, doc_tail, block_home, block_count
    )
    arrived = tie(arrived, rings[0].advance(first_done), down_ring.advance(finished))
    attended = tie(attend(table, arrived, group_heads, head_size), rings[0].advance(arrived))
    mixed = exchange_back(attended)
    third = rings[0].advance(attended)
    mixed = unpack(order, tie(mixed, down_ring.advance(attended)))

    reduced, unused_near, across = narrow_reduce(dot(mixed, out_weight))
    fourth = rings[0].advance(mixed)
    middle = inputs + tie(reduced, third)
    begun = rings[1].advance(across)
    normed_two, across = narrow_gather(row_normalize(middle, mlp_gain).astype(BF16))
    all_out_grad, unused_across = narrow_gather(tie(out_grad, mixed))
    normed_two = tie(normed_two, fourth, all_out_grad)
    second = rings[1].advance(across)
    down = down_ring.whole
    part = hidden // 2

    def half_forward(rows, weights):
        gate_sum, up_sum = dot(rows, weights[:, :part]), dot(rows, weights[:, part:])
        return gate_sum, up_sum, gated(gate_sum, up_sum).astype(BF16)

    def half_back(gate_sum, up_sum, grad_hidden):
        unused_gated, pull = jax.vjp(gated, gate_sum, up_sum)
        return jnp.concatenate([grad.astype(BF16) for grad in pull(grad_hidden)], axis=1)

    gate_sum, up_sum, hidden_first = half_forward(normed_two, rings[0].whole)
    wait_first = tie(all_out_grad, hidden_first, second)
    grad_first = half_back(gate_sum, up_sum, times_transpose(wait_first, down[:part]))
    third = rings[1].advance(hidden_first)
    first_half_terms = outer_sum(normed_two, tie(grad_first, third)).astype(BF16)
    first_half = Reduce(ring, first_half_terms)
    wait_second = tie(normed_two, first_half_terms, rings[1].advance(grad_first))
    gate_sum, up_sum, hidden_second = half_forward(wait_second, rings[1].whole)
    wait_second = tie(all_out_grad, hidden_second, first_half.advance())
    grad_second = half_back(gate_sum, up_sum, times_transpose(wait_second, down[part:]))
    grad_second = tie(grad_second, first_half.advance(hidden_second))
    early = first_half.advance(grad_second)
    grad_first = tie(grad_first, grad_second)
    grad_terms = (
        times_transpose(grad_first, rings[0].whole) + times_transpose(grad_second, rings[1].whole)
    ).astype(BF16)
    grad_terms = tie(grad_terms, early)
    grad_normed_two, near, across = narrow_reduce(grad_terms)
    third = first_half.advance(grad_terms)
    later_grad, later_normed, hidden_rows = tie(
        (grad_second, normed_two, (hidden_first, hidden_second)), near
    )
    hidden_rows = jnp.concatenate(hidden_rows, axis=1)
    second_half_terms = outer_sum(later_normed, later_grad).astype(BF16)
    second_half = Reduce(ring, second_half_terms)
    down_terms = outer_sum(hidden_rows, all_out_grad).astype(BF16)
    grad_normed_two = tie(grad_normed_two, third, second_half_terms, down_terms)
    unused_norm, second_pull = jax.vjp(lambda value: row_normalize(value, mlp_gain), middle)
    grad_middle = out_grad.astype(F32) + second_pull(grad_normed_two)[0]

    early = second_half.advance(across)
    grad_branch, across = narrow_gather(grad_middle.astype(BF16))
    grad_mixed = times_transpose(grad_branch, out_weight).astype(BF16)
    grad_pack = tie(pack(value_heads, order, grad_mixed), early, second_half.advance(across))
    third = second_half.advance(grad_pack)
    later_branch, later_hidden = tie((grad_branch, hidden_rows), grad_pack)
    arrived_grad = exchange(grad_pack)

    def narrow_rows(share):
        return narrow_exchange(share.astype(BF16).reshape(NARROW, shard, -1))

    last_sums = Reduce(ring, down_terms, outer_sum(mixed, later_branch).astype(BF16))
    arrived_grad = tie(arrived_grad, third, last_sums.advance())
    fourth = second_half.advance(arrived_grad)
    last_sums.advance(arrived_grad)
    grad_pieces = attend_back(table, arrived, arrived_grad, group_heads, head_size)
    grad_pieces = tie(grad_pieces, fourth)
    first_rows = narrow_rows(tie(first_half.result(), arrived_grad))
    output = (middle + narrow_reduce(dot(later_hidden, down))[0]).astype(BF16)
    second_rows = narrow_rows(tie(second_half.result(), grad_pieces))
    early = [last_sums.advance(grad_pieces), second_rows]
    grad_pieces = tie(exchange_back(grad_pieces), early, first_rows, output)
    projection_grad, norm_sums = unfinish(
        sizes, order, raw, grad_pieces, cosines, sines, norm_gains
    )
    first_terms = outer_sum(normed, projection_grad).astype(BF16)
    norm_terms = jnp.pad(
        norm_sums.astype(BF16), ((0, extra - 16), (0, projection_width - head_size))
    )
    first_sums = Reduce(ring, first_terms, shared=norm_terms)
    begun = first_sums.advance()
    grad_normed, near, across = narrow_reduce(
        times_transpose(tie(projection_grad, first_terms), projection)
    )
    fourth = last_sums.advance(begun)
    first_sums.advance(near)
    first_sums.advance(across, fourth)
    w_gate_grad, w_up_grad = merge_columns(block, first_rows, second_rows)
    first_sums.advance()
    unused_first, first_pull = jax.vjp(lambda value: row_normalize(value, attention_gain), inputs)
    tokens_grad = (grad_middle + first_pull(grad_normed)[0]).astype(BF16)

    def all_columns(pieces):
        return pieces.astype(F32).transpose(1, 0, 2).reshape(shard, -1)

    share = first_sums.result().astype(BF16)
    norm_rows = share[NARROW * shard :][:16]
    norm_rows = jnp.broadcast_to(norm_rows[None], (NARROW,) + norm_rows.shape)
    projection_rows = narrow_exchange(
        jnp.concatenate([share[: NARROW * shard].reshape(NARROW, shard, -1), norm_rows], axis=1)
    )
    norm_grads = jnp.sum(projection_rows[:, shard:, :head_size].astype(F32), axis=0)
    norm_grads = jnp.sum(norm_grads.reshape(2, 8, head_size), axis=1)
    projection_rows = projection_rows[:, :shard]
    w_query_grad = all_columns(projection_rows[:, :, :query_width])
    w_key_grad = all_columns(projection_rows[:, :, query_width : query_width + key_width])
    w_value_grad = all_columns(projection_rows[:, :, query_width + key_width :])
    last_share = last_sums.result()
    w_down_grad = last_share[:block]
    w_out_grad = lax.ppermute(last_share[block:].astype(BF16), DEVICES, moves_back).astype(F32)

    def row_sums(pairs):
        total = 0.0
        for weight, grad in pairs:
            total = total + jnp.sum(weight.astype(F32) * grad, axis=1)
        return total

    attn_norm_grad = row_sums(
        [(w_query, w_query_grad), (key_weight, w_key_grad), (value_weight, w_value_grad)]
    ) / attn_norm.astype(F32)
    mlp_norm_grad = row_sums([(w_gate, w_gate_grad), (w_up, w_up_grad)]) / mlp_norm.astype(F32)
    mine = lax.dynamic_slice(norm_grads, (0, (my_wide * NARROW + me) * few), (2, few))
    return (
        output,
        tokens_grad,
        attn_norm_grad,
        w_query_grad,
        w_key_grad,
        w_value_grad,
        mine[0],
        mine[1],
        w_out_grad,
        mlp_norm_grad,
        w_gate_grad,
        w_up_grad,
        w_down_grad,
    )


def solution(mesh):
    rows = P(DEVICES, None)
    vector = P(DEVICES)
    in_specs = (
        (rows, rows, vector, rows, rows, rows, vector, vector, rows, vector, rows, rows, rows)
        + (P(),) * 4
    )
    out_specs = (
        (rows, rows, vector, rows, rows, rows, vector, vector, rows, vector, rows, rows, rows)
    )
    return jax.shard_map(body, mesh=mesh, in_specs=in_specs, out_specs=out_specs, check_vma=False)
```

```python
import functools

import jax
import jax.numpy as jnp
import numpy as np
from jax import lax
from jax.experimental import pallas as pl
from jax.experimental.pallas import tpu as pltpu
from jax.sharding import PartitionSpec as P

BLK = 128
OWN_BLK = 4
EPSILON = 1e-06
THETA = 1000000.0
LANES = 128
NARROW = 4
CONTRACT_ROWS = (((0,), (0,)), ((), ()))
CONTRACT_COLS = (((1,), (1,)), ((), ()))
NEGATIVE = -1e30
F32 = jnp.float32
BF16 = jnp.bfloat16
DEVICES = ("wide", "narrow")


def row_normalize(values, gain_row):
    return (
        values * lax.rsqrt(jnp.mean(values * values, axis=-1, keepdims=True) + EPSILON) * gain_row
    )


def gated(gate_sum, up_sum):
    return jax.nn.silu(gate_sum) * up_sum


def dot(left, right):
    return jnp.dot(left, right, preferred_element_type=F32)


def outer_sum(left_rows, right_rows):
    return lax.dot_general(left_rows, right_rows, CONTRACT_ROWS, preferred_element_type=F32)


def times_transpose(left_rows, matrix):
    return lax.dot_general(left_rows, matrix, CONTRACT_COLS, preferred_element_type=F32)


def ring_order(count):
    rows = count // 2
    return [2 * i for i in range(rows)] + [2 * i + 1 for i in reversed(range(rows))]


class Ring:
    def __init__(self, count):
        self.count = count
        order = ring_order(count)
        place = np.zeros(count, np.int32)
        for i, device in enumerate(order):
            place[device] = i
        self.onward = [(order[i], order[(i + 1) % count]) for i in range(count)]
        self.back = [(b, a) for a, b in self.onward]
        self.order = jnp.asarray(np.array(order + order + order, np.int32))
        self.place = jnp.asarray(place)[lax.axis_index("wide")]

    def device(self, shift):
        return self.order[self.place + self.count + shift]

    def send(self, value, forward):
        return lax.ppermute(value, "wide", self.onward if forward else self.back)


def no_op(out_ref):
    pass


def blank(shape, dtype):
    return pl.pallas_call(
        no_op,
        out_shape=jax.ShapeDtypeStruct(shape, dtype),
        out_specs=pl.BlockSpec(memory_space=pl.ANY),
    )()


def tie(value, *after):
    after = [leaf for leaf in jax.tree.leaves(after)]
    return lax.optimization_barrier((value, after))[0] if after else value


class Gather:
    def __init__(self, ring, part):
        self.ring, self.rows, self.step, self.flight = ring, part.shape[0], 0, []
        self.ahead, self.behind = part, part
        if ring.count > 8:
            self.whole = lax.all_gather(part, "wide", axis=0, tiled=True)
        else:
            self.whole = self.put(
                blank((ring.count * self.rows, part.shape[1]), part.dtype), part, 0, 0
            )

    def put(self, whole, value, shift, extra):
        return lax.dynamic_update_slice(
            whole, value, (self.ring.device(shift) * self.rows + extra, 0)
        )

    def advance(self, *after):
        ring, half = self.ring, self.rows // 2
        if ring.count > 8:
            return []
        self.step += 1
        last = self.step == ring.count // 2
        ahead, behind = tie((self.ahead, self.behind), after)
        if last:
            ahead, behind = ahead[:half], behind[half:]
        self.ahead, self.behind = ring.send(ahead, True), ring.send(behind, False)
        self.whole = self.put(self.whole, self.ahead, -self.step, 0)
        self.whole = self.put(self.whole, self.behind, self.step, half if last else 0)
        return [self.ahead, self.behind]


class Reduce:
    def __init__(self, ring, *terms, shared=None):
        self.ring, self.terms, self.shared, self.step = ring, terms, shared, 0
        if ring.count > 8:
            parts = [term.reshape(ring.count, -1, term.shape[1]) for term in terms]
            if shared is not None:
                parts.append(jnp.broadcast_to(shared[None], (ring.count,) + shared.shape))
            whole = jnp.concatenate(parts, axis=1).reshape(-1, terms[0].shape[1])
            self.total = lax.psum_scatter(whole, "wide", scatter_dimension=0, tiled=True)

    def term(self, shift):
        parts = []
        for term in self.terms:
            rows = term.shape[0] // self.ring.count
            start = self.ring.device(shift) * rows
            parts.append(lax.dynamic_slice(term, (start, 0), (rows, term.shape[1])))
        if self.shared is not None:
            parts.append(self.shared)
        return parts[0] if len(parts) == 1 else jnp.concatenate(parts, axis=0)

    def advance(self, *after):
        ring = self.ring
        if ring.count > 8:
            return []
        shift = ring.count // 2 - self.step
        if self.step:
            ahead, behind = tie((self.ahead, self.behind), after)
            mine, other = self.term(shift), self.term(-shift)
            half = mine.shape[0] // 2
            if self.step == 1:
                ahead = jnp.concatenate([join(mine[:half], ahead), mine[half:]], axis=0)
                behind = jnp.concatenate([other[:half], join(other[half:], behind)], axis=0)
            else:
                ahead, behind = join(mine, ahead), join(other, behind)
        else:
            far = tie(self.term(shift), after)
            half = far.shape[0] // 2
            ahead, behind = far[:half], far[half:]
        self.step += 1
        self.ahead, self.behind = ring.send(ahead, True), ring.send(behind, False)
        return [self.ahead, self.behind]

    def result(self):
        if self.ring.count > 8:
            return self.total.astype(F32)
        return self.term(0).astype(F32) + self.ahead.astype(F32) + self.behind.astype(F32)


def join(left, right):
    return (left.astype(F32) + right.astype(F32)).astype(BF16)


def swap(value, bit):
    return lax.ppermute(value, "narrow", [(i, i ^ bit) for i in range(NARROW)])


def narrow_gather(value, across=None):
    across = swap(value, 2) if across is None else across
    return jnp.concatenate([value, swap(value, 1), across, swap(across, 1)], axis=0), across


def narrow_reduce(terms):
    rows = terms.shape[0] // NARROW
    low = terms.astype(BF16)
    parts = [low[i * rows : (i + 1) * rows] for i in range(NARROW)]
    near, far = swap(parts[1], 1), swap(parts[3], 1)
    across = swap(join(parts[2], far), 2)
    return parts[0].astype(F32) + near.astype(F32) + across.astype(F32), (near, far), across


def layout(doc_blocks, doc_order, block_home, my_wide, block_count):
    owners = doc_blocks.shape[1]
    owner_ids = jnp.arange(owners, dtype=jnp.int32)
    hits = (doc_order[:, :, None] == owner_ids[None, None, :]).astype(jnp.int32)
    in_stream = jnp.sum(hits * doc_blocks[:, None, :], axis=2)
    before = (owner_ids[:, None] < owner_ids[None, :]).astype(jnp.int32)
    stream_start = jnp.sum(in_stream[:, :, None] * before[None], axis=1)
    owner_start = jnp.sum(hits * stream_start[:, :, None], axis=1)
    column = jnp.sum(jnp.where(block_home == my_wide, owner_ids[None, :], 0), axis=1)
    stream_ids = jnp.arange(block_count, dtype=jnp.int32)[None, :] * owners + column[:, None]
    member = (owner_start[:, None, :] <= stream_ids[:, :, None]) & (
        stream_ids[:, :, None] < (owner_start + doc_blocks)[:, None, :]
    )
    offsets = stream_ids - jnp.sum(jnp.where(member, owner_start[:, None, :], 0), axis=2)
    return owner_start, offsets


def stream_table(group, owner_start, doc_blocks, doc_tail, block_home, block_count):
    def pick(table):
        return lax.dynamic_index_in_dim(table, group, 0, keepdims=False)

    starts, blocks, tails, homes = pick(owner_start), pick(doc_blocks), pick(doc_tail), pick(block_home)
    owners = starts.shape[0]
    ids = jnp.arange(owners * block_count, dtype=jnp.int32)
    member = (starts[None, :] <= ids[:, None]) & (ids[:, None] < (starts + blocks)[None, :])

    def chosen(values):
        return jnp.sum(jnp.where(member, values[None, :], 0), axis=1)

    home = jnp.sum(
        jnp.where(
            (ids % owners)[:, None] == jnp.arange(owners, dtype=jnp.int32)[None, :],
            homes[None, :],
            0,
        ),
        axis=1,
    )
    place = home * block_count + ids // owners
    return jnp.stack([place, chosen(starts), chosen((blocks - 1) * BLK + tails)])


def window(table, rows_ref, b, heads, size):
    first, length = table[1, b], table[2, b]
    width = heads * size
    mine = rows_ref[pl.ds(pl.multiple_of(table[0, b] * BLK, BLK), BLK), :width]
    queries = jnp.concatenate([mine[:, i * size : (i + 1) * size] for i in range(heads)], axis=0)
    spot = (b - first) * BLK
    row = lax.broadcasted_iota(jnp.int32, (heads, BLK, BLK), 1).reshape(heads * BLK, BLK) + spot
    col = lax.broadcasted_iota(jnp.int32, (heads * BLK, BLK), 1) + spot
    starts, keys, values, scores = [], [], [], []
    for i in range(OWN_BLK):
        start = pl.multiple_of(table[0, jnp.maximum(b - i, 0)] * BLK, BLK)
        key = rows_ref[pl.ds(start, BLK), width : width + size]
        col_i = col - i * BLK
        allowed = (col_i <= row) & (col_i < length) & (col_i >= 0)
        score = times_transpose(queries, key) * size ** (-0.5)
        starts.append(start)
        keys.append(key)
        values.append(rows_ref[pl.ds(start, BLK), width + size : width + 2 * size])
        scores.append(jnp.where(allowed, score, NEGATIVE))
    highest = scores[0]
    for score in scores[1:]:
        highest = jnp.maximum(highest, score)
    highest = jnp.max(highest, axis=-1, keepdims=True)
    powers = [jnp.exp(score - highest) for score in scores]
    total = powers[0]
    for power in powers[1:]:
        total = total + power
    total = jnp.sum(total, axis=-1, keepdims=True)
    weights = [power / total for power in powers]
    return mine, queries, starts, keys, values, weights


def forward_kernel(heads, size, table, rows_ref, out_ref):
    def step(b, carry):
        _, _, starts, _, values, weights = window(table, rows_ref, b, heads, size)
        mixed = dot(weights[0].astype(BF16), values[0])
        for weight, value in zip(weights[1:], values[1:]):
            mixed = mixed + dot(weight.astype(BF16), value)
        for i in range(heads):
            out_ref[pl.ds(starts[0], BLK), i * size : (i + 1) * size] = mixed[
                i * BLK : (i + 1) * BLK
            ].astype(BF16)
        return carry

    lax.fori_loop(0, table.shape[1], step, 0)


def backward_kernel(heads, size, table, rows_ref, grad_ref, out_ref, sums):
    sums[...] = jnp.zeros_like(sums)
    scale = size ** (-0.5)

    def step(b, carry):
        _, queries, starts, keys, values, weights = window(table, rows_ref, b, heads, size)
        grads = grad_ref[pl.ds(starts[0], BLK), :]
        grads = jnp.concatenate([grads[:, i * size : (i + 1) * size] for i in range(heads)], axis=0)
        pulls = [times_transpose(grads, value) for value in values]
        total = weights[0] * pulls[0]
        for weight, pull in zip(weights[1:], pulls[1:]):
            total = total + weight * pull
        total = jnp.sum(total, axis=-1, keepdims=True)
        grad_query = None
        for i in range(OWN_BLK):
            grad_score = (weights[i] * (pulls[i] - total)).astype(BF16)
            part = dot(grad_score, keys[i])
            grad_query = part if grad_query is None else grad_query + part
            spot = pl.ds(starts[i], BLK)
            sums[spot, :size] += outer_sum(grad_score, queries) * scale
            sums[spot, size:] += outer_sum(weights[i].astype(BF16), grads)
        for i in range(heads):
            out_ref[pl.ds(starts[0], BLK), i * size : (i + 1) * size] = (
                grad_query[i * BLK : (i + 1) * BLK] * scale
            ).astype(BF16)
        return carry

    lax.fori_loop(0, table.shape[1], step, 0)
    out_ref[:, heads * size :] = sums[...].astype(BF16)


def attend(table, rows, heads, size):
    return pl.pallas_call(
        functools.partial(forward_kernel, heads, size),
        out_shape=jax.ShapeDtypeStruct((rows.shape[0], heads * size), BF16),
        in_specs=[
            pl.BlockSpec(memory_space=pltpu.SMEM),
            pl.BlockSpec(memory_space=pltpu.VMEM),
        ],
        out_specs=pl.BlockSpec(memory_space=pltpu.VMEM),
        name="attend",
    )(table, rows)


def attend_back(table, rows, grads, heads, size):
    return pl.pallas_call(
        functools.partial(backward_kernel, heads, size),
        out_shape=jax.ShapeDtypeStruct(rows.shape, BF16),
        in_specs=[
            pl.BlockSpec(memory_space=pltpu.SMEM),
            pl.BlockSpec(memory_space=pltpu.VMEM),
            pl.BlockSpec(memory_space=pltpu.VMEM),
        ],
        out_specs=pl.BlockSpec(memory_space=pltpu.VMEM),
        scratch_shapes=[pltpu.VMEM((rows.shape[0], 2 * size), F32)],
        name="attend_back",
    )(table, rows, grads)


def unit_rows(values):
    return lax.rsqrt(jnp.mean(values * values, axis=-1, keepdims=True) + EPSILON)


def finish_kernel(sizes, order, raw_ref, cos_ref, sin_ref, gains_ref, out_ref):
    value_heads, group_heads, size = sizes
    per_group = group_heads * size
    query_width = value_heads * per_group
    key_width = value_heads * size

    def turned(start, gain):
        values = raw_ref[:, start : start + size]
        values = values * unit_rows(values) * gain
        return (
            values * cos_ref[...] + pltpu.roll(values, size // 2, 1) * sin_ref[...]
        ).astype(BF16)

    for head in range(value_heads):
        for i in range(group_heads):
            start = head * per_group + i * size
            out_ref[0, head, :, i * size : (i + 1) * size] = turned(start, gains_ref[0:1, :])
        start = query_width + head * size
        out_ref[0, head, :, per_group : per_group + size] = turned(start, gains_ref[1:2, :])
        start = query_width + key_width + head * size
        out_ref[0, head, :, per_group + size :] = raw_ref[:, start : start + size].astype(BF16)


def unfinish_kernel(
    sizes, order, raw_ref, grad_ref, cos_ref, sin_ref, gains_ref, out_ref, sums_ref
):
    value_heads, group_heads, size = sizes
    per_group = group_heads * size
    query_width = value_heads * per_group
    key_width = value_heads * size

    @pl.when(pl.program_id(0) == 0)
    def _():
        sums_ref[...] = jnp.zeros_like(sums_ref)

    def pull(grad, start, which):
        grad = grad.astype(F32)
        values = raw_ref[:, start : start + size]
        unit = unit_rows(values)
        values = values * unit
        grad = grad * cos_ref[...] + pltpu.roll(grad * sin_ref[...], size // 2, 1)
        sums_ref[which * 8 : which * 8 + 8, :] += jnp.sum(
            (grad * values).reshape(-1, 8, size), axis=0
        )
        grad = grad * gains_ref[which : which + 1, :]
        grad = unit * (grad - values * jnp.mean(grad * values, axis=-1, keepdims=True))
        out_ref[:, start : start + size] = grad.astype(BF16)

    for head in range(value_heads):
        for i in range(group_heads):
            pull(
                grad_ref[0, head, :, i * size : (i + 1) * size], head * per_group + i * size, 0
            )
        pull(grad_ref[0, head, :, per_group : per_group + size], query_width + head * size, 1)
        start = query_width + key_width + head * size
        out_ref[:, start : start + size] = grad_ref[0, head, :, per_group + size :]


def pack_kernel(heads, order, rows_ref, out_ref):
    width = out_ref.shape[3]
    for head in range(heads):
        out_ref[0, head] = rows_ref[:, head * width : (head + 1) * width]


def unpack_kernel(heads, order, pieces_ref, out_ref):
    width = pieces_ref.shape[3]
    for head in range(heads):
        out_ref[:, head * width : (head + 1) * width] = pieces_ref[0, head]


def row_spec(rows, cols):
    return pl.BlockSpec((rows, cols), lambda i, order: (i, 0))


def whole_spec(shape):
    return pl.BlockSpec(shape, lambda i, order: (0,) * len(shape))


def piece_spec(heads, rows, cols):
    return pl.BlockSpec((1, heads, rows, cols), lambda i, order: (order[i], 0, 0, 0))


def by_rows(kernel, name, order, args, in_specs, out_shape, out_specs, cost):
    return pl.pallas_call(
        kernel,
        grid_spec=pltpu.PrefetchScalarGridSpec(
            num_scalar_prefetch=1, grid=(NARROW,), in_specs=in_specs, out_specs=out_specs
        ),
        out_shape=out_shape,
        cost_estimate=pl.CostEstimate(flops=cost, bytes_accessed=cost, transcendentals=0),
        name=name,
    )(order, *args)


def finish(sizes, order, raw, cosines, sines, gains):
    value_heads, group_heads, size = sizes
    rows = raw.shape[0] // NARROW
    width = (group_heads + 2) * size
    return by_rows(
        functools.partial(finish_kernel, sizes),
        "finish",
        order,
        (raw, cosines, sines, gains),
        [
            row_spec(rows, raw.shape[1]),
            row_spec(rows, size),
            row_spec(rows, size),
            whole_spec(gains.shape),
        ],
        jax.ShapeDtypeStruct((NARROW, value_heads, rows, width), BF16),
        piece_spec(value_heads, rows, width),
        8 << 20,
    )


def unfinish(sizes, order, raw, pieces, cosines, sines, gains):
    value_heads, group_heads, size = sizes
    rows = raw.shape[0] // NARROW
    return by_rows(
        functools.partial(unfinish_kernel, sizes),
        "unfinish",
        order,
        (raw, pieces, cosines, sines, gains),
        [
            row_spec(rows, raw.shape[1]),
            piece_spec(value_heads, rows, pieces.shape[3]),
            row_spec(rows, size),
            row_spec(rows, size),
            whole_spec(gains.shape),
        ],
        (
            jax.ShapeDtypeStruct(raw.shape, BF16),
            jax.ShapeDtypeStruct((16, size), F32),
        ),
        (row_spec(rows, raw.shape[1]), whole_spec((16, size))),
        8 << 20,
    )


def pack(heads, order, values):
    rows = values.shape[0] // NARROW
    width = values.shape[1] // heads
    return by_rows(
        functools.partial(pack_kernel, heads),
        "pack",
        order,
        (values,),
        [row_spec(rows, values.shape[1])],
        jax.ShapeDtypeStruct((NARROW, heads, rows, width), BF16),
        piece_spec(heads, rows, width),
        2 << 20,
    )


def unpack(order, pieces):
    heads, rows, width = pieces.shape[1:]
    return by_rows(
        functools.partial(unpack_kernel, heads),
        "unpack",
        order,
        (pieces,),
        [piece_spec(heads, rows, width)],
        jax.ShapeDtypeStruct((NARROW * rows, heads * width), BF16),
        row_spec(rows, heads * width),
        2 << 20,
    )


def split_kernel(block, gate_ref, up_ref, out_ref):
    places = gate_ref.shape[1] // (block * NARROW)
    half = out_ref.shape[2] // 2
    for i, ref in enumerate((gate_ref, up_ref)):
        for n in range(NARROW):
            for place in range(places):
                chunk, spot = divmod(place, places // 2)
                start = chunk * half + i * (half // 2) + spot * block
                source = (place * NARROW + n) * block
                out_ref[n, :, start : start + block] = ref[:, source : source + block]


def merge_kernel(block, first_ref, second_ref, gate_ref, up_ref):
    places = gate_ref.shape[1] // (block * NARROW)
    half = first_ref.shape[2]
    for i, ref in enumerate((gate_ref, up_ref)):
        for n in range(NARROW):
            for place in range(places):
                chunk, spot = divmod(place, places // 2)
                source = (first_ref, second_ref)[chunk]
                start = i * (half // 2) + spot * block
                target = (place * NARROW + n) * block
                ref[:, target : target + block] = source[n, :, start : start + block].astype(F32)


def split_columns(block, gate, up):
    rows, cols = gate.shape
    if block % 64:
        def by_chunk(values):
            values = values.reshape(rows, 2, -1, NARROW, block).transpose(3, 0, 1, 2, 4)
            return values.reshape(NARROW, rows, 2, -1)

        both = jnp.concatenate([by_chunk(gate), by_chunk(up)], axis=3)
        return both.reshape(NARROW, rows, -1)
    return pl.pallas_call(
        functools.partial(split_kernel, block),
        out_shape=jax.ShapeDtypeStruct((NARROW, rows, 2 * cols // NARROW), BF16),
        name="split_columns",
    )(gate, up)


def merge_columns(block, first, second):
    rows, half = first.shape[1:]
    cols = half * NARROW
    if block % 64:
        both = jnp.stack([first, second], axis=2).reshape(NARROW, rows, 2, 2, -1, block)
        both = both.transpose(3, 1, 2, 4, 0, 5).reshape(2, rows, cols).astype(F32)
        return both[0], both[1]
    return pl.pallas_call(
        functools.partial(merge_kernel, block),
        out_shape=(jax.ShapeDtypeStruct((rows, cols), F32),) * 2,
        name="merge_columns",
    )(first, second)


def body(
    tokens,
    out_grad,
    attn_norm,
    w_query,
    key_weight,
    value_weight,
    query_norm,
    key_norm_gain,
    w_out,
    mlp_norm,
    w_gate,
    w_up,
    w_down,
    doc_blocks,
    doc_tail,
    doc_order,
    block_home,
):
    wide_count = lax.axis_size("wide")
    my_wide = lax.axis_index("wide")
    me = lax.axis_index("narrow")
    device_count = wide_count * NARROW
    ring = Ring(wide_count)
    rows = tokens.shape[0]
    block_count = rows // BLK
    head_size = query_norm.shape[0] * device_count
    query_width = w_query.shape[1] // NARROW
    key_width = key_weight.shape[1] // NARROW
    value_heads = key_width // head_size
    group_heads = query_width // key_width
    hidden = w_gate.shape[1] // NARROW
    shard = w_query.shape[0]
    parts = wide_count // (NARROW * value_heads)

    order = me ^ jnp.arange(NARROW, dtype=jnp.int32)
    sizes = (value_heads, group_heads, head_size)

    def narrow_exchange(pieces):
        pieces = jnp.take(pieces, order, axis=0)
        moved = [pieces[0]] + [swap(pieces[i], i) for i in range(1, NARROW)]
        return jnp.take(jnp.stack(moved), order, axis=0)

    def narrow_columns(weight):
        return weight.reshape(shard, NARROW, -1).transpose(1, 0, 2)

    def pad_lanes(values, size):
        return jnp.concatenate([values, jnp.zeros((size - values.shape[0],), BF16)])

    projection_width = query_width + 2 * key_width
    gains = [pad_lanes(gain, shard) for gain in (attn_norm, mlp_norm, query_norm, key_norm_gain)]
    gains = pad_lanes(jnp.concatenate(gains), projection_width)[None, :]
    extra = 32
    at_row = lax.broadcasted_iota(jnp.int32, (extra, projection_width), 0) == me
    gain_rows = jnp.broadcast_to(jnp.where(at_row, gains, 0)[None], (NARROW, extra, projection_width))
    first_pieces = jnp.concatenate(
        [narrow_columns(w_query), narrow_columns(key_weight), narrow_columns(value_weight)], axis=2
    )
    first_pieces = narrow_exchange(jnp.concatenate([first_pieces, gain_rows], axis=1))
    tokens_across = swap(tokens, 2)
    moves = [(g, (g % wide_count) * NARROW + g // wide_count) for g in range(device_count)]
    moves_back = [(b, a) for a, b in moves]
    out_part = lax.ppermute(w_out, DEVICES, moves)
    folds = w_out.shape[1] // projection_width
    out_part = out_part.reshape(shard, folds, -1).transpose(1, 0, 2).reshape(folds * shard, -1)
    gain_rows = jnp.sum(first_pieces[:, shard:].astype(F32), axis=0).astype(BF16)
    first_part = jnp.concatenate(
        [first_pieces[:, :shard].reshape(NARROW * shard, -1), out_part, gain_rows], axis=0
    )
    block = w_down.shape[0]
    first_ring = Gather(ring, first_part)
    down_ring = Gather(ring, w_down)
    begun = first_ring.advance(down_ring.advance())
    first_ring.advance(tokens_across)
    gate_part, up_part = tie((w_gate, w_up), begun)
    gate_up_pieces = split_columns(block, gate_part, up_part)
    gate_up_part = narrow_exchange(gate_up_pieces).reshape(NARROW * shard, -1)
    first_ring.advance()
    first_done = first_ring.advance()
    gathered = first_ring.whole.reshape(wide_count, -1, projection_width)
    projection = gathered[:, : NARROW * shard].reshape(-1, projection_width)
    out_rows = gathered[:, NARROW * shard : (NARROW + folds) * shard]
    out_rows = out_rows.reshape(wide_count, folds, shard, -1).transpose(0, 2, 1, 3)
    out_weight = out_rows.reshape(wide_count * shard, -1)
    gain_rows = gathered[:, (NARROW + folds) * shard :][:, :NARROW, : 4 * shard]
    gain_rows = gain_rows.reshape(device_count, 4, shard).astype(F32)
    attention_gain, mlp_gain = gain_rows[:, 0].reshape(-1), gain_rows[:, 1].reshape(-1)
    few = query_norm.shape[0]
    norm_gains = jnp.stack(
        [gain_rows[:, 2, :few].reshape(head_size), gain_rows[:, 3, :few].reshape(head_size)]
    )
    norm_gains = jnp.concatenate([norm_gains, jnp.zeros((6, head_size), F32)])
    rings = [Gather(ring, gate_up_part[:, :hidden]), Gather(ring, gate_up_part[:, hidden:])]

    inputs = tokens.astype(F32)
    all_inputs = narrow_gather(tokens, tokens_across)[0].astype(F32)
    normed = row_normalize(all_inputs, attention_gain).astype(BF16)
    raw = dot(normed, projection)
    owner_start, offsets = layout(
        doc_blocks, doc_order, tie(block_home, begun), my_wide, block_count
    )
    my_offsets = jnp.take(offsets, order, axis=0)
    position = (
        my_offsets.reshape(-1, 1) * BLK + jnp.arange(BLK, dtype=jnp.int32)[None, :]
    ).reshape(-1)
    half_size = head_size // 2
    frequency = THETA ** (-2.0 * jnp.arange(half_size, dtype=F32) / head_size)
    angles = position.astype(F32)[:, None] * frequency[None, :]
    cosines, sines = jnp.cos(angles), jnp.sin(angles)
    cosines = jnp.concatenate([cosines, cosines], axis=-1)
    sines = jnp.concatenate([-sines, sines], axis=-1)

    def exchange(pieces):
        pieces = jnp.broadcast_to(
            pieces[:, :, None], pieces.shape[:2] + (parts,) + pieces.shape[2:]
        ).reshape(wide_count, rows, -1)
        return lax.all_to_all(pieces, "wide", split_axis=0, concat_axis=0, tiled=True).reshape(
            wide_count * rows, -1
        )

    def exchange_back(values):
        pieces = lax.all_to_all(
            values.reshape(wide_count, rows, -1), "wide", split_axis=0, concat_axis=0, tiled=True
        )
        return pieces.reshape(NARROW, value_heads, parts, rows, -1)[:, :, 0]

    finished = finish(sizes, order, raw, cosines, sines, norm_gains)
    arrived = exchange(tie(finished, down_ring.advance(first_done)))
    table = stream_table(
        my_wide // (wide_count // NARROW), owner_start, doc_blocks, doc_tail, block_home, block_count
    )
    arrived = tie(arrived, rings[0].advance(first_done), down_ring.advance(finished))
    attended = tie(attend(table, arrived, group_heads, head_size), rings[0].advance(arrived))
    mixed = exchange_back(attended)
    third = rings[0].advance(attended)
    mixed = unpack(order, tie(mixed, down_ring.advance(attended)))

    reduced, unused_near, across = narrow_reduce(dot(mixed, out_weight))
    fourth = rings[0].advance(mixed)
    middle = inputs + tie(reduced, third)
    begun = rings[1].advance(across)
    normed_two, across = narrow_gather(row_normalize(middle, mlp_gain).astype(BF16))
    all_out_grad, unused_across = narrow_gather(tie(out_grad, mixed))
    normed_two = tie(normed_two, fourth, all_out_grad)
    second = rings[1].advance(across)
    down = down_ring.whole
    part = hidden // 2

    def half_forward(rows, weights):
        gate_sum, up_sum = dot(rows, weights[:, :part]), dot(rows, weights[:, part:])
        return gate_sum, up_sum, gated(gate_sum, up_sum).astype(BF16)

    def half_back(gate_sum, up_sum, grad_hidden):
        unused_gated, pull = jax.vjp(gated, gate_sum, up_sum)
        return jnp.concatenate([grad.astype(BF16) for grad in pull(grad_hidden)], axis=1)

    gate_sum, up_sum, hidden_first = half_forward(normed_two, rings[0].whole)
    wait_first = tie(all_out_grad, hidden_first, second)
    grad_first = half_back(gate_sum, up_sum, times_transpose(wait_first, down[:part]))
    third = rings[1].advance(hidden_first)
    first_half_terms = outer_sum(normed_two, tie(grad_first, third)).astype(BF16)
    first_half = Reduce(ring, first_half_terms)
    wait_second = tie(normed_two, first_half_terms, rings[1].advance(grad_first))
    gate_sum, up_sum, hidden_second = half_forward(wait_second, rings[1].whole)
    wait_second = tie(all_out_grad, hidden_second, first_half.advance())
    grad_second = half_back(gate_sum, up_sum, times_transpose(wait_second, down[part:]))
    early = first_half.advance(hidden_second)
    grad_first = tie(grad_first, grad_second)
    grad_terms = (
        times_transpose(grad_first, rings[0].whole) + times_transpose(grad_second, rings[1].whole)
    ).astype(BF16)
    grad_terms = tie(grad_terms, early)
    grad_normed_two, near, across = narrow_reduce(grad_terms)
    third = first_half.advance(grad_terms)
    later_grad, later_normed, hidden_rows = tie(
        (grad_second, normed_two, (hidden_first, hidden_second)), near
    )
    hidden_rows = jnp.concatenate(hidden_rows, axis=1)
    second_half_terms = outer_sum(later_normed, later_grad).astype(BF16)
    second_half = Reduce(ring, second_half_terms)
    down_terms = outer_sum(hidden_rows, all_out_grad).astype(BF16)
    grad_normed_two = tie(grad_normed_two, third, second_half_terms, down_terms)
    unused_norm, second_pull = jax.vjp(lambda value: row_normalize(value, mlp_gain), middle)
    grad_middle = out_grad.astype(F32) + second_pull(grad_normed_two)[0]

    early = [first_half.advance(across), second_half.advance(across)]
    grad_branch, across = narrow_gather(grad_middle.astype(BF16))
    grad_mixed = times_transpose(grad_branch, out_weight).astype(BF16)
    grad_pack = tie(pack(value_heads, order, grad_mixed), early)
    second = second_half.advance(across)
    later_branch, later_hidden = tie((grad_branch, hidden_rows), grad_pack)
    arrived_grad = exchange(grad_pack)

    def narrow_rows(share):
        return narrow_exchange(share.astype(BF16).reshape(NARROW, shard, -1))

    last_sums = Reduce(ring, down_terms, outer_sum(mixed, later_branch).astype(BF16))
    arrived_grad = tie(arrived_grad, second, last_sums.advance())
    third = second_half.advance(arrived_grad)
    grad_pieces = attend_back(table, arrived, arrived_grad, group_heads, head_size)
    grad_pieces = tie(grad_pieces, third)
    first_rows = narrow_rows(tie(first_half.result(), arrived_grad))
    output = (middle + narrow_reduce(dot(later_hidden, down))[0]).astype(BF16)
    early = [second_half.advance(grad_pieces), last_sums.advance(grad_pieces)]
    grad_pieces = tie(exchange_back(grad_pieces), early, first_rows, output)
    projection_grad, norm_sums = unfinish(
        sizes, order, raw, grad_pieces, cosines, sines, norm_gains
    )
    first_terms = outer_sum(normed, projection_grad).astype(BF16)
    norm_terms = jnp.pad(
        norm_sums.astype(BF16), ((0, extra - 16), (0, projection_width - head_size))
    )
    first_sums = Reduce(ring, first_terms, shared=norm_terms)
    begun = first_sums.advance()
    grad_normed, near, across = narrow_reduce(
        times_transpose(tie(projection_grad, first_terms), projection)
    )
    second_rows = narrow_rows(tie(second_half.result(), begun))
    third = last_sums.advance(begun)
    begun = first_sums.advance(near)
    last_sums.advance(begun)
    first_sums.advance(across, third)
    w_gate_grad, w_up_grad = merge_columns(block, first_rows, second_rows)
    first_sums.advance(second_rows)
    unused_first, first_pull = jax.vjp(lambda value: row_normalize(value, attention_gain), inputs)
    tokens_grad = (grad_middle + first_pull(grad_normed)[0]).astype(BF16)

    def all_columns(pieces):
        return pieces.astype(F32).transpose(1, 0, 2).reshape(shard, -1)

    share = first_sums.result().astype(BF16)
    norm_rows = share[NARROW * shard :][:16]
    norm_rows = jnp.broadcast_to(norm_rows[None], (NARROW,) + norm_rows.shape)
    projection_rows = narrow_exchange(
        jnp.concatenate([share[: NARROW * shard].reshape(NARROW, shard, -1), norm_rows], axis=1)
    )
    norm_grads = jnp.sum(projection_rows[:, shard:, :head_size].astype(F32), axis=0)
    norm_grads = jnp.sum(norm_grads.reshape(2, 8, head_size), axis=1)
    projection_rows = projection_rows[:, :shard]
    w_query_grad = all_columns(projection_rows[:, :, :query_width])
    w_key_grad = all_columns(projection_rows[:, :, query_width : query_width + key_width])
    w_value_grad = all_columns(projection_rows[:, :, query_width + key_width :])
    last_share = last_sums.result()
    w_down_grad = last_share[:block]
    w_out_grad = lax.ppermute(last_share[block:].astype(BF16), DEVICES, moves_back).astype(F32)

    def row_sums(pairs):
        total = 0.0
        for weight, grad in pairs:
            total = total + jnp.sum(weight.astype(F32) * grad, axis=1)
        return total

    attn_norm_grad = row_sums(
        [(w_query, w_query_grad), (key_weight, w_key_grad), (value_weight, w_value_grad)]
    ) / attn_norm.astype(F32)
    mlp_norm_grad = row_sums([(w_gate, w_gate_grad), (w_up, w_up_grad)]) / mlp_norm.astype(F32)
    mine = lax.dynamic_slice(norm_grads, (0, (my_wide * NARROW + me) * few), (2, few))
    return (
        output,
        tokens_grad,
        attn_norm_grad,
        w_query_grad,
        w_key_grad,
        w_value_grad,
        mine[0],
        mine[1],
        w_out_grad,
        mlp_norm_grad,
        w_gate_grad,
        w_up_grad,
        w_down_grad,
    )


def solution(mesh):
    rows = P(DEVICES, None)
    vector = P(DEVICES)
    in_specs = (
        (rows, rows, vector, rows, rows, rows, vector, vector, rows, vector, rows, rows, rows)
        + (P(),) * 4
    )
    out_specs = (
        (rows, rows, vector, rows, rows, rows, vector, vector, rows, vector, rows, rows, rows)
    )
    return jax.shard_map(body, mesh=mesh, in_specs=in_specs, out_specs=out_specs, check_vma=False)
```
